128 devices in a mesh: tm: 8 (over y_hi, z), rows: 16 (over y_lo, x, core).
Axes of the slice: x: 4, y: 4 (y_hi: 2, y_lo: 2; y = y_hi * 2 + y_lo), z: 4, core: 2. Of those that a mesh axis runs over, the one named last changes fastest.
Arguments:
- video: bfloat16 [1, 32, 128, 128, 256], P(None, 'tm', 'rows'), may hold values from -6 to 6
- spatial_weight: bfloat16 [2304, 256], P(('tm', 'rows')), may hold values from -0.125 to 0.125
- temporal_weight: bfloat16 [768, 256], P(('tm', 'rows')), may hold values from -0.21875 to 0.21875
- cotangent: bfloat16 [1, 32, 128, 128, 256], P(None, 'tm', 'rows'), may hold values from -6 to 6
Outputs:
- output: bfloat16 [1, 32, 128, 128, 256], P(None, 'tm', 'rows')
- grad_video: bfloat16 [1, 32, 128, 128, 256], P(None, 'tm', 'rows')
- grad_spatial: float32 [2304, 256], P(('tm', 'rows'))
- grad_temporal: float32 [768, 256], P(('tm', 'rows'))
The draws below stay inside these ranges and needn't reach their ends.
All inputs are finite; a program needn't handle non-finite values.
Results may differ from the reference program's by a relative error of at most 0.0053.
Values may be sent and summed in bfloat16 or wider, within the bound.
No kernel may reach another device: no remote copies, remote signals or barrier semaphores. Data moves between devices by JAX's collectives and lax.ppermute only.
A program may use at most 128 MiB of HBM per device.

```python
import jax
import jax.numpy as jnp
from jax import lax

C = 256
BATCH = 1
COLS = 128
FRAMES = 32
HEIGHT = 128


def spiked(drawn, stream_key, source, target, parts, factor):
    def block_of(axis_at):
        return (jnp.arange(drawn.shape[axis_at]) // (drawn.shape[axis_at] // parts)).reshape((-1,) + (1,) * (drawn.ndim - 1 - axis_at))

    one_side = jax.random.permutation(stream_key, parts)[block_of(target)]
    far = (block_of(target) + parts // 2) % parts
    return jnp.where((block_of(source) == one_side) | (block_of(source) == far), factor * drawn, drawn)


def steps_of(key, shape, cuts, low, largest):
    level = 1.0
    for axis_at, parts in cuts:
        heights = jax.random.uniform(jax.random.fold_in(jax.random.fold_in(key, 6), axis_at), (parts,), jnp.float32, low / len(cuts), largest / len(cuts))
        level = level * jnp.repeat(jnp.exp(heights), shape[axis_at] // parts).reshape((-1,) + (1,) * (len(shape) - 1 - axis_at))
    return level


def gaussian(rng, dims, scale, reach, cuts=(), kind=jnp.bfloat16):
    gain = steps_of(rng, dims, cuts, -0.22, 0.18) if cuts else 1.0
    values = jax.random.normal(rng, dims, jnp.float32) * scale * gain
    return jnp.minimum(jnp.maximum(values, -reach), reach).astype(kind)


def bell_draw_with(stream_key, shape, scale, bound, cuts, heavy, kind=jnp.bfloat16):
    array = scale * jax.random.normal(stream_key, shape, jnp.float32)
    if cuts:
        array = array * steps_of(stream_key, shape, cuts, -0.22, 0.18)
    return jnp.clip(spiked(array, jax.random.fold_in(stream_key, 3), *heavy), -bound, bound).astype(kind)


def setup_inputs(seed: int = 0) -> dict:
    arg_keys = jax.random.split(jax.random.key(seed), 5)
    video = gaussian(arg_keys[0], (BATCH, FRAMES, HEIGHT, COLS, C), 1.0, 6.0, ((1, 8), (2, 16)))
    spatial_weight = gaussian(arg_keys[1], (9 * C, C), (9 * C) ** -0.5, 0.125, ((0, 128),))
    temporal_weight = gaussian(arg_keys[2], (3 * C, C), (3 * C) ** -0.5, 0.21875, ((0, 128),))
    cotangent = bell_draw_with(arg_keys[3], (BATCH, FRAMES, HEIGHT, COLS, C), 1.0, 6.0, ((1, 8), (2, 16)), (2, 4, 16, 2.0))
    return dict(video=video, spatial_weight=spatial_weight, temporal_weight=temporal_weight, cotangent=cotangent)


epsilon = 1e-06

def spatial_cols(field):
    padded = jnp.pad(field, ((1, 1), (1, 1), (0, 0)))
    n_rows, n_cols = (field.shape[0], field.shape[1])
    pieces = [padded[i:i + n_rows, j:j + n_cols] for i in range(3) for j in range(3)]
    return jnp.concatenate(pieces, axis=-1).reshape(n_rows * n_cols, -1)

def silu_slope(value):
    sigmoid = jax.nn.sigmoid(value)
    return sigmoid * (1.0 + value * (1.0 - sigmoid))

def contract(left, right):
    return lax.dot_general(left, right, (((0,), (0,)), ((), ())), preferred_element_type=jnp.float32)

def normalize(one_frame):
    values = one_frame.astype(jnp.float32)
    inv_rms = lax.rsqrt(lax.optimization_barrier(jnp.mean(values * values, axis=-1, keepdims=True)) + epsilon)
    return (values * inv_rms, inv_rms)

def reverse_spatial(weight, chans):
    return weight.reshape(3, 3, chans, chans)[::-1, ::-1].transpose(0, 1, 3, 2).reshape(9 * chans, chans)

def reverse_temporal(weight, chans):
    return weight.reshape(3, chans, chans)[::-1].transpose(0, 2, 1).reshape(3 * chans, chans)

def reference(video, spatial_weight, temporal_weight, cotangent):
    n_batch, n_frames, n_rows, n_cols, chans = video.shape
    flat_video = video.reshape(n_batch * n_frames, n_rows, n_cols, chans)

    def forward_frame(one_frame):
        normed, inv_rms = normalize(one_frame)
        activated = jax.nn.silu(normed).astype(jnp.bfloat16)
        pre_act = jnp.dot(spatial_cols(activated), spatial_weight, preferred_element_type=jnp.float32)
        return (activated, pre_act.reshape(n_rows, n_cols, chans))
    activated, pre_act = lax.map(forward_frame, flat_video)
    hidden = jax.nn.silu(pre_act).astype(jnp.bfloat16).reshape(n_batch, n_frames, n_rows, n_cols, chans)
    blank = jnp.zeros((n_batch, 2, n_rows, n_cols, chans), jnp.bfloat16)
    past = jnp.concatenate([blank, hidden], axis=1)
    ahead = jnp.concatenate([cotangent, blank], axis=1)
    back_temporal = reverse_temporal(temporal_weight, chans)

    def temporal_frame(carry, frame_idx):
        from_past = jnp.concatenate([lax.dynamic_index_in_dim(past, frame_idx + k, 1, keepdims=False) for k in range(3)], axis=-1).reshape(-1, 3 * chans)
        from_ahead = jnp.concatenate([lax.dynamic_index_in_dim(ahead, frame_idx + k, 1, keepdims=False) for k in range(3)], axis=-1).reshape(-1, 3 * chans)
        grad_out = lax.dynamic_index_in_dim(cotangent, frame_idx, 1, keepdims=False).reshape(-1, chans)
        mixed = jnp.dot(from_past, temporal_weight, preferred_element_type=jnp.float32)
        back = jnp.dot(from_ahead, back_temporal, preferred_element_type=jnp.float32)
        return (carry + contract(from_past, grad_out), (mixed, back))
    grad_temporal, (mixed, back) = lax.scan(temporal_frame, jnp.zeros((3 * chans, chans), jnp.float32), jnp.arange(n_frames, dtype=jnp.int32))
    mixed = mixed.reshape(n_frames, n_batch, n_rows, n_cols, chans).transpose(1, 0, 2, 3, 4)
    back = back.reshape(n_frames, n_batch, n_rows, n_cols, chans).transpose(1, 0, 2, 3, 4)
    output = (video.astype(jnp.float32) + mixed).astype(jnp.bfloat16)
    grad_pre = (back.reshape(n_batch * n_frames, n_rows, n_cols, chans) * silu_slope(pre_act)).astype(jnp.bfloat16)
    back_spatial = reverse_spatial(spatial_weight, chans)
    flat_grad = cotangent.reshape(n_batch * n_frames, n_rows, n_cols, chans)

    def spatial_back(carry, items):
        one_frame, act_frame, pre_grad, grad_frame = items
        normed, inv_rms = normalize(one_frame)
        grad_act = jnp.dot(spatial_cols(pre_grad), back_spatial, preferred_element_type=jnp.float32).reshape(n_rows, n_cols, chans)
        grad_norm = grad_act * silu_slope(normed)
        grad_in = inv_rms * (grad_norm - normed * lax.optimization_barrier(jnp.mean(grad_norm * normed, axis=-1, keepdims=True)))
        result = (grad_frame.astype(jnp.float32) + grad_in).astype(jnp.bfloat16)
        return (carry + contract(spatial_cols(act_frame), pre_grad.reshape(-1, chans)), result)
    grad_spatial, grad_video = lax.scan(spatial_back, jnp.zeros((9 * chans, chans), jnp.float32), (flat_video, activated, grad_pre, flat_grad))
    factor = float(n_batch * n_frames * n_rows * n_cols) ** (-0.5)
    grad_video = grad_video.reshape(n_batch, n_frames, n_rows, n_cols, chans)
    return (output, grad_video, grad_spatial * factor, grad_temporal * factor)
```

```python
import functools

import jax
import jax.numpy as jnp
from jax import lax
from jax.experimental import pallas as pl
from jax.experimental.pallas import tpu as pltpu
from jax.sharding import PartitionSpec as P

epsilon = 1e-06
F32, BF16 = jnp.float32, jnp.bfloat16
AXES = ("tm", "rows")


def place(d):
    return d // 64, (d // 16) % 4, (d // 8) % 2, (d // 2) % 4, d % 2


def number(yh, z, yl, x, c):
    return ((yh * 4 + z) * 2 + yl) * 8 + x * 2 + c


def shift(axis, by):
    pairs = []
    for d in range(128):
        yh, z, yl, x, c = place(d)
        if axis == "core":
            c = (c + by) % 2
        elif axis == "x":
            x = (x + by) % 4
        elif axis == "z":
            z = (z + by) % 4
        else:
            y = (yh * 2 + yl + by) % 4
            yh, yl = y // 2, y % 2
        pairs.append((d, number(yh, z, yl, x, c)))
    return pairs


def moved(value, axis, by):
    return lax.ppermute(value, AXES, shift(axis, by))


def gathered_axis(value, axis, mine):
    buf = jnp.zeros((4,) + value.shape, value.dtype)
    for by in (1, 2, 3):
        buf = lax.dynamic_update_index_in_dim(buf, moved(value, axis, by), (mine - by) % 4, 0)
    return lax.dynamic_update_index_in_dim(buf, value, mine, 0)


def scattered_axis(value, axis, mine):
    total = lax.dynamic_index_in_dim(value, mine, 0, keepdims=False)
    for by in (1, 2, 3):
        part = lax.dynamic_index_in_dim(value, (mine + by) % 4, 0, keepdims=False)
        total = total + moved(part, axis, by)
    return total


def both_kernels(spatial, temporal, at):
    y, z, x, c = at
    chans = spatial.shape[1]
    rows_s, rows_t = spatial.shape[0], temporal.shape[0]
    own = jnp.concatenate([spatial, temporal], axis=0)
    other = moved(own, "core", 1)
    pair = jnp.where(c == 0, jnp.stack([own, other]), jnp.stack([other, own]))
    unit = gathered_axis(pair, "x", x).reshape(8, rows_s + rows_t, chans)
    unit = jnp.concatenate(
        [unit[:, :rows_s].reshape(8 * rows_s, chans), unit[:, rows_s:].reshape(8 * rows_t, chans)]
    )
    half_rows = 4 * (rows_s + rows_t)
    half = lax.dynamic_slice_in_dim(unit, c * half_rows, half_rows, 0)
    half = gathered_axis(half, "z", z)
    half = gathered_axis(half, "y", y)
    other = moved(half, "core", 1)
    low = jnp.where(c == 0, half, other)
    high = jnp.where(c == 0, other, half)
    units = jnp.concatenate([low, high], axis=2)
    units = units.reshape(2, 2, 4, 2 * half_rows, chans).transpose(0, 2, 1, 3, 4)
    units = units.reshape(16, 2 * half_rows, chans)
    return (
        units[:, : 8 * rows_s].reshape(128 * rows_s, chans),
        units[:, 8 * rows_s :].reshape(128 * rows_t, chans),
    )


def summed_kernels(grad_s, grad_t, at):
    y, z, x, c = at
    chans = grad_s.shape[1]
    rows_s, rows_t = grad_s.shape[0] // 128, grad_t.shape[0] // 128
    half_rows = 4 * (rows_s + rows_t)
    units = jnp.concatenate(
        [grad_s.reshape(16, 8 * rows_s, chans), grad_t.reshape(16, 8 * rows_t, chans)], axis=1
    )
    halves = units.reshape(16, 2, half_rows, chans)
    keep = lax.dynamic_index_in_dim(halves, c, 1, keepdims=False)
    send = lax.dynamic_index_in_dim(halves, 1 - c, 1, keepdims=False)
    half = keep + moved(send, "core", 1)
    half = half.reshape(2, 4, 2, half_rows, chans).transpose(0, 2, 1, 3, 4)
    half = half.reshape(4, 4, half_rows, chans)
    half = scattered_axis(half, "y", y)
    half = scattered_axis(half, "z", z)
    other = moved(half, "core", 1)
    unit = jnp.concatenate([jnp.where(c == 0, half, other), jnp.where(c == 0, other, half)])
    blocks = jnp.concatenate(
        [
            unit[: 8 * rows_s].reshape(4, 2, rows_s, chans),
            unit[8 * rows_s :].reshape(4, 2, rows_t, chans),
        ],
        axis=2,
    )
    blocks = lax.dynamic_index_in_dim(blocks, c, 1, keepdims=False)
    mine = scattered_axis(blocks, "x", x)
    return mine[:rows_s], mine[rows_s:]


def edge_rows(value):
    count = lax.axis_size("rows")
    up = [(i, i + 1) for i in range(count - 1)]
    down = [(j, i) for i, j in up]
    return (
        lax.ppermute(value[:, -1:], "rows", up),
        lax.ppermute(value[:, :1], "rows", down),
    )


def along_frames(value, by):
    count = lax.axis_size("tm")
    pairs = [(i, i + by) for i in range(count) if 0 <= i + by < count]
    return lax.ppermute(value, "tm", pairs)


def sigmoid(value):
    return 1.0 / (1.0 + jnp.exp(-value))


def dot(left, right):
    return jnp.dot(left, right, preferred_element_type=F32)


def contract(left, right):
    return lax.dot_general(left, right, (((0,), (0,)), ((), ())), preferred_element_type=F32)


def normalize(cells):
    inv_rms = lax.rsqrt(jnp.mean(cells * cells, axis=-1, keepdims=True) + epsilon)
    return cells * inv_rms, inv_rms


def store_shifts(out, row, value):
    cols, chans = value.shape
    col = lax.broadcasted_iota(jnp.int32, value.shape, 0)
    before = jnp.where(col == 0, 0.0, pltpu.roll(value, 1, 0))
    after = jnp.where(col == cols - 1, 0.0, pltpu.roll(value, cols - 1, 0))
    out[row, :, :chans] = before.astype(BF16)
    out[row, :, chans : 2 * chans] = value.astype(BF16)
    out[row, :, 2 * chans :] = after.astype(BF16)


def activate_kernel(video, above, below, shifts):
    n_rows = video.shape[1]
    for row in range(n_rows + 2):
        cells = above[0, 0] if row == 0 else below[0, 0] if row > n_rows else video[0, row - 1]
        normed, _ = normalize(cells.astype(F32))
        store_shifts(shifts.at[0], row, normed * sigmoid(normed))


def forward_kernel(shifts, cot0, cot1, cot2, w_s, w_back, hidden, grad_pre):
    _, n_rows, n_cols, chans = hidden.shape
    step = 4
    for row in range(0, n_rows, step):
        pre = None
        for tap in range(3):
            left = shifts[0, row + tap : row + tap + step].reshape(step * n_cols, 3 * chans)
            term = dot(left, w_s[3 * chans * tap : 3 * chans * (tap + 1)])
            pre = term if pre is None else pre + term
        back = None
        for k, cot in enumerate((cot0, cot1, cot2)):
            left = cot[0, row : row + step].reshape(step * n_cols, chans)
            term = dot(left, w_back[chans * k : chans * (k + 1)])
            back = term if back is None else back + term
        gate = sigmoid(pre)
        hidden[0, row : row + step] = (pre * gate).astype(BF16).reshape(step, n_cols, chans)
        slope = gate * (1.0 + pre * (1.0 - gate))
        grad_pre[0, row : row + step] = (back * slope).astype(BF16).reshape(step, n_cols, chans)


def weights_kernel(shifts, grad_pre, hidden, cot0, cot1, cot2, grad_s, grad_t):
    @pl.when(pl.program_id(0) == 0)
    def _():
        grad_s[...] = jnp.zeros_like(grad_s)
        grad_t[...] = jnp.zeros_like(grad_t)

    _, n_rows, n_cols, chans = hidden.shape
    cells = n_rows * n_cols
    right = grad_pre[0].reshape(cells, chans)
    for tap in range(3):
        left = shifts[0, tap : tap + n_rows].reshape(cells, 3 * chans)
        grad_s[3 * chans * tap : 3 * chans * (tap + 1)] += contract(left, right)
    left = hidden[0].reshape(cells, chans)
    for k, cot in enumerate((cot2, cot1, cot0)):
        grad_t[chans * k : chans * (k + 1)] += contract(left, cot[0].reshape(cells, chans))


def backward_kernel(grad_pre, above, below, video, cot, w_rev, grad_video, shifts):
    _, n_rows, n_cols, chans = video.shape
    for row in range(n_rows + 2):
        cells = above[0, 0] if row == 0 else below[0, 0] if row > n_rows else grad_pre[0, row - 1]
        store_shifts(shifts, row, cells.astype(F32))
    step = 4
    for row in range(0, n_rows, step):
        grad_act = None
        for tap in range(3):
            left = shifts[row + tap : row + tap + step].reshape(step * n_cols, 3 * chans)
            term = dot(left, w_rev[3 * chans * tap : 3 * chans * (tap + 1)])
            grad_act = term if grad_act is None else grad_act + term
        cells = video[0, row : row + step].reshape(step * n_cols, chans).astype(F32)
        normed, inv_rms = normalize(cells)
        gate = sigmoid(normed)
        grad_norm = grad_act * (gate * (1.0 + normed * (1.0 - gate)))
        along = jnp.mean(grad_norm * normed, axis=-1, keepdims=True)
        grad_in = inv_rms * (grad_norm - normed * along)
        total = cot[0, row : row + step].reshape(step * n_cols, chans).astype(F32) + grad_in
        grad_video[0, row : row + step] = total.astype(BF16).reshape(step, n_cols, chans)


def output_kernel(video, hid0, hid1, hid2, past0, past1, w_t, output):
    frame = pl.program_id(0)
    _, n_rows, n_cols, chans = video.shape
    step = 4
    for row in range(0, n_rows, step):
        rows = slice(row, row + step)
        mixed = dot(hid2[0, rows].reshape(step * n_cols, chans), w_t[2 * chans :])
        first = jnp.where(frame < 2, past0[0, rows], hid0[0, rows]).reshape(step * n_cols, chans)
        mixed += dot(first, w_t[:chans])
        second = jnp.where(frame < 1, past1[0, rows], hid1[0, rows]).reshape(step * n_cols, chans)
        mixed += dot(second, w_t[chans : 2 * chans])
        cells = video[0, rows].reshape(step * n_cols, chans).astype(F32)
        output[0, rows] = (cells + mixed).astype(BF16).reshape(step, n_cols, chans)


def frame_spec(shape, index=lambda f: f):
    return pl.BlockSpec((1,) + tuple(shape[1:]), lambda f: (index(f), 0, 0, 0))


def whole(shape):
    return pl.BlockSpec(tuple(shape), lambda f: (0, 0), pipeline_mode=pl.Buffered(1))


def call(body, n_frames, in_specs, out_specs, out_shape, flops, scratch=()):
    return pl.pallas_call(
        body,
        grid=(n_frames,),
        in_specs=in_specs,
        out_specs=out_specs,
        out_shape=out_shape,
        scratch_shapes=scratch,
        cost_estimate=pl.CostEstimate(flops=flops, bytes_accessed=8 << 20, transcendentals=0),
        compiler_params=pltpu.CompilerParams(vmem_limit_bytes=56 << 20),
    )


def reverse_spatial(weight, chans):
    return (
        weight.reshape(3, 3, chans, chans)[::-1, ::-1]
        .transpose(0, 1, 3, 2)
        .reshape(9 * chans, chans)
    )


def reverse_temporal(weight, chans):
    return weight.reshape(3, chans, chans)[::-1].transpose(0, 2, 1).reshape(3 * chans, chans)


def shards(video, spatial_weight, temporal_weight, cotangent):
    _, n_frames, n_rows, n_cols, chans = video.shape
    t, r = lax.axis_index("tm"), lax.axis_index("rows")
    at = ((t // 4) * 2 + r // 8, t % 4, (r // 2) % 4, r % 2)
    video, cot = video[0], cotangent[0]
    shape = (n_frames, n_rows, n_cols, chans)
    wide = (n_frames, n_rows + 2, n_cols, 3 * chans)
    edge = (n_frames, 1, n_cols, chans)
    pair = 2 * n_frames * n_rows * n_cols * chans * chans

    above, below = edge_rows(video)
    shifts = call(
        activate_kernel,
        n_frames,
        [frame_spec(shape), frame_spec(edge), frame_spec(edge)],
        frame_spec(wide),
        jax.ShapeDtypeStruct(wide, BF16),
        pair // 8,
    )(video, above, below)
    w_s, w_t = both_kernels(spatial_weight, temporal_weight, at)
    ahead = along_frames(cot[:2], -1)
    cots = jnp.concatenate([cot, ahead], axis=0)
    cot_specs = [frame_spec(shape, lambda f, k=k: f + k) for k in range(3)]
    hidden, grad_pre = call(
        forward_kernel,
        n_frames,
        [frame_spec(wide)] + cot_specs + [whole(w_s.shape), whole(w_t.shape)],
        [frame_spec(shape)] * 2,
        [jax.ShapeDtypeStruct(shape, BF16)] * 2,
        12 * pair,
    )(shifts, cots, cots, cots, w_s, reverse_temporal(w_t, chans))
    past = along_frames(hidden[n_frames - 2 :], 1)
    above, below = edge_rows(grad_pre)
    grad_s, grad_t = call(
        weights_kernel,
        n_frames,
        [frame_spec(wide), frame_spec(shape), frame_spec(shape)] + cot_specs,
        [whole((9 * chans, chans)), whole((3 * chans, chans))],
        [
            jax.ShapeDtypeStruct((9 * chans, chans), F32),
            jax.ShapeDtypeStruct((3 * chans, chans), F32),
        ],
        12 * pair,
    )(shifts, grad_pre, hidden, cots, cots, cots)
    grad_video = call(
        backward_kernel,
        n_frames,
        [frame_spec(shape), frame_spec(edge), frame_spec(edge), frame_spec(shape)]
        + [frame_spec(shape), whole(w_s.shape)],
        frame_spec(shape),
        jax.ShapeDtypeStruct(shape, BF16),
        9 * pair,
        [pltpu.VMEM(wide[1:], BF16)],
    )(grad_pre, above, below, video, cot, reverse_spatial(w_s, chans))
    output = call(
        output_kernel,
        n_frames,
        [
            frame_spec(shape),
            frame_spec(shape, lambda f: jnp.maximum(f - 2, 0)),
            frame_spec(shape, lambda f: jnp.maximum(f - 1, 0)),
            frame_spec(shape),
            frame_spec(shape, lambda f: jnp.minimum(f, 1)),
            frame_spec(shape, lambda f: 1),
            whole(w_t.shape),
        ],
        frame_spec(shape),
        jax.ShapeDtypeStruct(shape, BF16),
        3 * pair,
    )(video, hidden, hidden, hidden, past, past, w_t)
    spatial_part, temporal_part = summed_kernels(grad_s, grad_t, at)
    total_cells = n_frames * n_rows * n_cols * lax.axis_size("tm") * lax.axis_size("rows")
    factor = float(total_cells) ** (-0.5)
    return (output[None], grad_video[None], spatial_part * factor, temporal_part * factor)


def solution(mesh):
    cells = P(None, "tm", "rows", None, None)
    kernels = P(("tm", "rows"), None)
    return jax.shard_map(
        shards,
        mesh=mesh,
        in_specs=(cells, kernels, kernels, cells),
        out_specs=(cells, cells, kernels, kernels),
        check_vma=False,
    )
```

```python
import jax
import jax.numpy as jnp
import numpy as np
from jax import lax
from jax.experimental import pallas as pl
from jax.experimental.pallas import tpu as pltpu
from jax.sharding import PartitionSpec as P


epsilon = 1e-06
F32, BF16 = jnp.float32, jnp.bfloat16
AXES = ("tm", "rows")


def place(d):
    return d // 64, (d // 16) % 4, (d // 8) % 2, (d // 2) % 4, d % 2


def number(yh, z, yl, x, c):
    return ((yh * 4 + z) * 2 + yl) * 8 + x * 2 + c


def ring(axis):
    pairs = []
    for d in range(128):
        yh, z, yl, x, c = place(d)
        by = 1 - 2 * c
        if axis == "core":
            c = 1 - c
        elif axis == "x":
            x = (x + by) % 4
        elif axis == "z":
            z = (z + by) % 4
        else:
            y = (yh * 2 + yl + by) % 4
            yh, yl = y // 2, y % 2
        pairs.append((d, number(yh, z, yl, x, c)))
    return pairs


def moved(value, axis):
    return lax.ppermute(value, AXES, ring(axis))


def put(buf, part, *index):
    index = tuple(index) + (0,) * (buf.ndim - len(index))
    return lax.dynamic_update_slice(buf, part.reshape((1,) * (buf.ndim - part.ndim) + part.shape), index)


def take(value, index):
    return lax.dynamic_index_in_dim(value, index, 0, keepdims=False)


def gathered_axis(value, axis, mine, core):
    way = 1 - 2 * core
    full = moved(value, axis)
    half = moved(take(full, core), axis)
    other_full = moved(full, "core")
    other_half = moved(half, "core")
    buf = jnp.zeros((4,) + value.shape, value.dtype)
    buf = put(buf, value, mine)
    buf = put(buf, full, (mine - way) % 4)
    buf = put(buf, other_full, (mine + way) % 4)
    buf = put(buf, half, (mine + 2) % 4, core)
    return put(buf, other_half, (mine + 2) % 4, 1 - core)


def scattered_ring(own, send_half, keep_half, send_full, keep_full, axis, core):
    half = keep_half + moved(send_half, "core")
    full = keep_full + moved(send_full, "core")
    passed = moved(half, axis)
    full = put(full, take(full, core) + passed, core)
    return own + moved(full, axis)


def ring_blocks(value, mine, core):
    way = 1 - 2 * core
    opposite = take(value, (mine + 2) % 4)
    return (
        take(value, mine),
        take(opposite, 1 - core),
        take(opposite, core),
        take(value, (mine - way) % 4),
        take(value, (mine + way) % 4),
    )


def both_kernels(spatial, temporal, at):
    y, z, x, c = at
    chans = spatial.shape[1]
    rows_s, rows_t = spatial.shape[0], temporal.shape[0]
    own = jnp.concatenate([spatial, temporal], axis=0)
    other = moved(own, "core")
    pair = put(put(jnp.zeros((2,) + own.shape, own.dtype), own, c), other, 1 - c)
    rows = rows_s + rows_t
    units = gathered_axis(pair, "z", z, c)
    units = gathered_axis(units.reshape(2, 4 * rows, chans), "y", y, c)
    units = gathered_axis(units.reshape(2, 16 * rows, chans), "x", x, c)
    return units.reshape(4, 4, 4, 2 * rows, chans)


def unit_order(rows_s, rows_t):
    rows = rows_s + rows_t
    source = [rows * block + row for block in range(8) for row in range(rows_s)]
    source += [rows * block + rows_s + row for block in range(8) for row in range(rows_t)]
    return np.eye(8 * rows, dtype=np.float32)[source]


def summed_kernels(blocks, rows_s, rows_t, at):
    _, z, x, c = at
    chans = blocks[0].shape[-1]
    rows = 8 * (rows_s + rows_t)
    total = scattered_ring(*blocks, "y", c)
    total = total.reshape(4, 2, rows // 2, chans)
    total = scattered_ring(*ring_blocks(total, z, c), "z", c).reshape(rows, chans)
    total = jnp.concatenate(
        [
            total[: 8 * rows_s].reshape(4, 2, rows_s, chans),
            total[8 * rows_s :].reshape(4, 2, rows_t, chans),
        ],
        axis=2,
    )
    total = scattered_ring(*ring_blocks(total, x, c), "x", c)
    mine = take(total, c) + moved(take(total, 1 - c), "core")
    return mine[:rows_s], mine[rows_s:]


def traded_edges(inner, outer):
    count = lax.axis_size("rows")
    pairs = [(r, r + (1 if r % 2 else -1)) for r in range(count)]
    pairs = [(r, s) for r, s in pairs if 0 <= s < count]
    outer = lax.ppermute(outer, "rows", pairs)
    return moved(inner, "core"), outer


def edge_rows(value, core):
    last = value.shape[1] - 1
    inner = lax.dynamic_slice_in_dim(value, last * (1 - core), 1, 1)
    outer = lax.dynamic_slice_in_dim(value, last * core, 1, 1)
    return traded_edges(inner, outer)


def along_frames(value, by):
    count = lax.axis_size("tm")
    pairs = [(i, i + by) for i in range(count) if 0 <= i + by < count]
    return lax.ppermute(value, "tm", pairs)


def sigmoid(value):
    return 1.0 / (1.0 + jnp.exp(-value))


def dot(left, right):
    return jnp.dot(left, right, preferred_element_type=F32)


def contract(left, right):
    return lax.dot_general(left, right, (((0,), (0,)), ((), ())), preferred_element_type=F32)


def normalize(cells):
    inv_rms = lax.rsqrt(jnp.mean(cells * cells, axis=-1, keepdims=True) + epsilon)
    return cells * inv_rms, inv_rms


def store_shifts(out, row, value):
    cols, chans = value.shape
    col = lax.broadcasted_iota(jnp.int32, value.shape, 0)
    before = jnp.where(col == 0, 0.0, pltpu.roll(value, 1, 0))
    after = jnp.where(col == cols - 1, 0.0, pltpu.roll(value, cols - 1, 0))
    out[row, :, :chans] = before.astype(BF16)
    out[row, :, chans : 2 * chans] = value.astype(BF16)
    out[row, :, 2 * chans :] = after.astype(BF16)


def halo_row(row, n_rows, core, inner, outer, body):
    if row == 0:
        return jnp.where(core == 0, outer[0, 0], inner[0, 0])
    if row > n_rows:
        return jnp.where(core == 0, inner[0, 0], outer[0, 0])
    return body[0, row - 1]


def activate_kernel(at, video, inner, outer, _, shifts):
    n_rows = video.shape[1]
    for row in range(n_rows + 2):
        cells = halo_row(row, n_rows, at[1], inner, outer, video)
        normed, _ = normalize(cells.astype(F32))
        store_shifts(shifts.at[0], row, normed * sigmoid(normed))


def unit_number(y, z):
    return ((y // 2) * 4 + z) * 2 + y % 2


def assemble_kernel(order, units, w_s, w_t, w_back):
    chans = w_s.shape[1]
    rows_s, rows_t = w_s.shape[0] // 16, w_t.shape[0] // 16
    for y in range(4):
        for z in range(4):
            u = unit_number(y, z)
            blocks = jnp.concatenate([units[x, y, z] for x in range(4)], axis=0)
            unit = dot(order[...], blocks).astype(BF16)
            w_s[rows_s * u : rows_s * (u + 1)] = unit[:rows_s]
            w_t[rows_t * u : rows_t * (u + 1)] = unit[rows_s:]
    for k in range(3):
        w_back[chans * k : chans * (k + 1)] = w_t[chans * (2 - k) : chans * (3 - k)].T


def reverse_kernel(w_s, w_rev):
    chans = w_s.shape[1]
    for k in range(9):
        w_rev[chans * k : chans * (k + 1)] = w_s[chans * (8 - k) : chans * (9 - k)].T


def cot_window(frame, cot0, cot1, cot2, ahead1, ahead2, rows, last):
    return (
        cot0[0, rows],
        jnp.where(frame >= last, ahead1[0, rows], cot1[0, rows]),
        jnp.where(frame >= last - 1, ahead2[0, rows], cot2[0, rows]),
    )


def forward_kernel(
    at, shifts, cot0, cot1, cot2, ahead1, ahead2, w_s, w_back, hidden, grad_pre, inner, outer
):
    _, n_rows, n_cols, chans = hidden.shape
    step, frame = 4, at[2] + pl.program_id(0)
    for row in range(0, n_rows, step):
        pre = None
        for tap in range(3):
            left = shifts[0, row + tap : row + tap + step].reshape(step * n_cols, 3 * chans)
            term = dot(left, w_s[3 * chans * tap : 3 * chans * (tap + 1)])
            pre = term if pre is None else pre + term
        back = None
        window = cot_window(
            frame, cot0, cot1, cot2, ahead1, ahead2, slice(row, row + step), at[3]
        )
        for k, cot in enumerate(window):
            left = cot.reshape(step * n_cols, chans)
            term = dot(left, w_back[chans * k : chans * (k + 1)])
            back = term if back is None else back + term
        gate = sigmoid(pre)
        hidden[0, row : row + step] = (pre * gate).astype(BF16).reshape(step, n_cols, chans)
        slope = gate * (1.0 + pre * (1.0 - gate))
        grad_pre[0, row : row + step] = (back * slope).astype(BF16).reshape(step, n_cols, chans)
    first, final = grad_pre[0, 0], grad_pre[0, n_rows - 1]
    inner[0, 0] = jnp.where(at[1] == 0, final, first)
    outer[0, 0] = jnp.where(at[1] == 0, first, final)


def weights_kernel(
    at, shifts, grad_pre, hidden, cot0, cot1, cot2, ahead1, ahead2,
    own, send_half, keep_half, send_full, keep_full, grad_s, grad_t,
):
    @pl.when(pl.program_id(0) == 0)
    def _():
        grad_s[...] = jnp.zeros_like(grad_s)
        grad_t[...] = jnp.zeros_like(grad_t)

    _, n_rows, n_cols, chans = hidden.shape
    cells = n_rows * n_cols
    last = pl.num_programs(0) - 1
    frame = pl.program_id(0)
    right = grad_pre[0].reshape(cells, chans)
    for tap in range(3):
        left = shifts[0, tap : tap + n_rows].reshape(cells, 3 * chans)
        grad_s[3 * chans * tap : 3 * chans * (tap + 1)] += contract(left, right)
    left = hidden[0].reshape(cells, chans)
    window = cot_window(frame, cot0, cot1, cot2, ahead1, ahead2, slice(0, n_rows), last)
    for k, cot in enumerate(window[::-1]):
        grad_t[chans * k : chans * (k + 1)] += contract(left, cot.reshape(cells, chans))

    @pl.when(pl.program_id(0) == last)
    def _():
        rows_s, rows_t = 9 * chans // 16, 3 * chans // 16
        mine, core = at[0], at[1]
        way = 1 - 2 * core

        def fill(out, index, y, z):
            u = unit_number(y, z)
            top = (index % 2) * (rows_s + rows_t)
            at_s = pl.ds(pl.multiple_of(rows_s * u, rows_t), rows_s)
            at_t = pl.ds(pl.multiple_of(rows_t * u, rows_t), rows_t)
            target = out if out.ndim == 2 else out.at[index // 2]
            target[top : top + rows_s] = grad_s[at_s]
            target[top + rows_s : top + rows_s + rows_t] = grad_t[at_t]

        for z in range(4):
            fill(own, z, mine, z)
            fill(send_full, z, lax.rem(mine + 4 - way, 4), z)
            fill(keep_full, z, lax.rem(mine + 4 + way, 4), z)
        opposite = lax.rem(mine + 2, 4)
        for z in range(2):
            fill(send_half, z, opposite, 2 * (1 - core) + z)
            fill(keep_half, z, opposite, 2 * core + z)


def backward_kernel(at, grad_pre, inner, outer, video, cot, w_rev, _, grad_video, shifts):
    _, n_rows, n_cols, chans = video.shape
    for row in range(n_rows + 2):
        cells = halo_row(row, n_rows, at[1], inner, outer, grad_pre)
        store_shifts(shifts, row, cells.astype(F32))
    step = 4
    for row in range(0, n_rows, step):
        grad_act = None
        for tap in range(3):
            left = shifts[row + tap : row + tap + step].reshape(step * n_cols, 3 * chans)
            term = dot(left, w_rev[3 * chans * tap : 3 * chans * (tap + 1)])
            grad_act = term if grad_act is None else grad_act + term
        cells = video[0, row : row + step].reshape(step * n_cols, chans).astype(F32)
        normed, inv_rms = normalize(cells)
        gate = sigmoid(normed)
        grad_norm = grad_act * (gate * (1.0 + normed * (1.0 - gate)))
        along = jnp.mean(grad_norm * normed, axis=-1, keepdims=True)
        grad_in = inv_rms * (grad_norm - normed * along)
        total = cot[0, row : row + step].reshape(step * n_cols, chans).astype(F32) + grad_in
        grad_video[0, row : row + step] = total.astype(BF16).reshape(step, n_cols, chans)


def output_kernel(at, video, past0, past1, hid0, hid1, hid2, w_t, _, output):
    frame = pl.program_id(0)
    _, n_rows, n_cols, chans = video.shape
    step = 4
    for row in range(0, n_rows, step):
        rows = slice(row, row + step)
        parts = (
            jnp.where(frame < 2, past0[0, rows], hid0[0, rows]),
            jnp.where(frame < 1, past1[0, rows], hid1[0, rows]),
            hid2[0, rows],
        )
        left = jnp.concatenate([part.reshape(step * n_cols, chans) for part in parts], axis=-1)
        cells = video[0, rows].reshape(step * n_cols, chans).astype(F32)
        mixed = dot(left, w_t[...])
        output[0, rows] = (cells + mixed).astype(BF16).reshape(step, n_cols, chans)


def frame_spec(shape, index=lambda f: f):
    return pl.BlockSpec((1,) + tuple(shape[1:]), lambda f, *_: (index(f), 0, 0, 0))


def whole(shape):
    return pl.BlockSpec(
        tuple(shape), lambda f, *_: (0,) * len(shape), pipeline_mode=pl.Buffered(1)
    )


def call(
    body, n_frames, in_specs, out_specs, out_shape, flops, scratch=(), scalars=0, aliases={},
    limit=20,
):
    return pl.pallas_call(
        body,
        grid_spec=pltpu.PrefetchScalarGridSpec(
            num_scalar_prefetch=scalars,
            grid=(n_frames,),
            in_specs=in_specs,
            out_specs=out_specs,
            scratch_shapes=scratch,
        ),
        out_shape=out_shape,
        input_output_aliases=aliases,
        cost_estimate=pl.CostEstimate(flops=flops, bytes_accessed=8 << 20, transcendentals=0),
        compiler_params=pltpu.CompilerParams(vmem_limit_bytes=limit << 20),
    )


def part_of(body, part, parts, specs, out, args, flops, scratch=(), before=None):
    count = out.shape[0] // parts
    base = part * count
    in_specs = []
    for shape, index in specs:
        if index is None:
            in_specs.append(whole(shape))
        else:
            in_specs.append(frame_spec(shape, lambda f, g=index: g(f, base)))
    if before is None:
        in_specs.append(pl.BlockSpec(memory_space=pltpu.SMEM))
        before, aliases = jnp.zeros((1,), jnp.int32), {}
    else:
        in_specs.append(pl.BlockSpec(memory_space=pl.ANY))
        aliases = {len(args): 0}
    return call(
        body,
        count,
        in_specs,
        frame_spec(out.shape, lambda f: f + base),
        out,
        flops // parts,
        scratch,
        1,
        aliases,
    )(*args, before)


def single(body, out_shapes, flops, *args, limit=12):
    return pl.pallas_call(
        body,
        in_specs=[pl.BlockSpec(memory_space=pltpu.VMEM)] * len(args),
        out_specs=[pl.BlockSpec(memory_space=pltpu.VMEM)] * len(out_shapes),
        out_shape=[jax.ShapeDtypeStruct(shape, BF16) for shape in out_shapes],
        cost_estimate=pl.CostEstimate(flops=flops, bytes_accessed=3 << 20, transcendentals=0),
        compiler_params=pltpu.CompilerParams(vmem_limit_bytes=limit << 20),
    )(*args)


def residual_block(video, spatial_weight, temporal_weight, cotangent):
    _, n_frames, n_rows, n_cols, chans = video.shape
    t, r = lax.axis_index("tm"), lax.axis_index("rows")
    y, z, x, core = at = ((t // 4) * 2 + r // 8, t % 4, (r // 2) % 4, r % 2)
    video, cot = video[0], cotangent[0]
    shape = (n_frames, n_rows, n_cols, chans)
    wide = (n_frames, n_rows + 2, n_cols, 3 * chans)
    edge = (n_frames, 1, n_cols, chans)
    count = n_frames // 2
    half = (count,) + shape[1:]
    pair = 2 * n_frames * n_rows * n_cols * chans * chans
    rows_s, rows_t = spatial_weight.shape[0], temporal_weight.shape[0]
    rows = 8 * (rows_s + rows_t)
    last = n_frames - 1
    at_part = [jnp.stack([y, core, base, last]).astype(jnp.int32) for base in (0, count)]
    same = lambda f, base: f + base

    ahead = along_frames(cot[:2], -1)
    inner, outer = edge_rows(video, core)
    units = both_kernels(spatial_weight, temporal_weight, at)
    shifts = None
    for part in range(2):
        shifts = part_of(
            activate_kernel,
            part,
            2,
            [(shape, same), (edge, same), (edge, same)],
            jax.ShapeDtypeStruct(wide, BF16),
            (at_part[part], video, inner, outer),
            pair,
            before=shifts,
        )
    full_s, full_t = (9 * chans, chans), (3 * chans, chans)
    order = jnp.asarray(unit_order(rows_s, rows_t), BF16)
    w_s, w_t, w_back = single(assemble_kernel, (full_s, full_t, full_t), pair // 4, order, units)
    (w_rev,) = single(reverse_kernel, (full_s,), pair // 4, w_s)

    def cot_specs(base):
        specs = [
            frame_spec(shape, lambda f, k=k: jnp.minimum(f + base + k, last)) for k in range(3)
        ]
        return specs + [
            frame_spec(half, lambda f, k=k: jnp.maximum(f + base + k - last - 1, 0)) for k in (1, 2)
        ]

    hidden, grad_pre, edge_in, edge_out = call(
        forward_kernel,
        n_frames,
        [frame_spec(wide)] + cot_specs(0) + [whole(full_s), whole(full_t)],
        [frame_spec(shape)] * 2 + [frame_spec(edge)] * 2,
        [jax.ShapeDtypeStruct(shape, BF16)] * 2 + [jax.ShapeDtypeStruct(edge, BF16)] * 2,
        12 * pair,
        scalars=1,
    )(at_part[0], shifts, cot, cot, cot, ahead, ahead, w_s, w_back)
    edges = traded_edges(edge_in, edge_out)
    past = along_frames(hidden[count:], 1)
    block, half_block = (2, 2 * rows, chans), (2 * rows, chans)
    block_shapes = (block, half_block, half_block, block, block)
    blocks = call(
        weights_kernel,
        n_frames,
        [frame_spec(wide), frame_spec(shape), frame_spec(shape)] + cot_specs(0),
        [whole(shape_) for shape_ in block_shapes],
        [jax.ShapeDtypeStruct(shape_, F32) for shape_ in block_shapes],
        12 * pair,
        [pltpu.VMEM(full_s, F32), pltpu.VMEM(full_t, F32)],
        scalars=1,
        limit=28,
    )(at_part[0], shifts, grad_pre, hidden, cot, cot, cot, ahead, ahead)
    grad_video = part_of(
        backward_kernel,
        0,
        1,
        [(shape, same), (edge, same), (edge, same), (shape, same), (shape, same), (full_s, None)],
        jax.ShapeDtypeStruct(shape, BF16),
        (at_part[0], grad_pre, *edges, video, cot, w_rev),
        9 * pair,
        [pltpu.VMEM(wide[1:], BF16)],
    )
    output = part_of(
        output_kernel,
        0,
        1,
        [
            (shape, same),
            (half, lambda f, base: jnp.minimum(f, count - 1)),
            (half, lambda f, base: count - 1),
            (shape, lambda f, base: jnp.maximum(f - 2, 0)),
            (shape, lambda f, base: jnp.maximum(f - 1, 0)),
            (shape, same),
            (full_t, None),
        ],
        jax.ShapeDtypeStruct(shape, BF16),
        (at_part[0], video, past, past, hidden, hidden, hidden, w_t),
        3 * pair,
    )
    spatial_part, temporal_part = summed_kernels(blocks, rows_s, rows_t, at)
    total_cells = n_frames * n_rows * n_cols * lax.axis_size("tm") * lax.axis_size("rows")
    factor = float(total_cells) ** (-0.5)
    return (output[None], grad_video[None], spatial_part * factor, temporal_part * factor)


def solution(mesh):
    cells = P(None, "tm", "rows", None, None)
    kernels = P(("tm", "rows"), None)
    return jax.shard_map(
        residual_block,
        mesh=mesh,
        in_specs=(cells, kernels, kernels, cells),
        out_specs=(cells, cells, kernels, kernels),
        check_vma=False,
    )
```

```python
import jax
import jax.numpy as jnp
import numpy as np
from jax import lax
from jax.experimental import pallas as pl
from jax.experimental.pallas import tpu as pltpu
from jax.sharding import Mesh
from jax.sharding import PartitionSpec as P


epsilon = 1e-06
F32, BF16 = jnp.float32, jnp.bfloat16
FRAME_AXES, ROW_AXES = ("y_hi", "z"), ("y_lo", "x", "core")
AXES = FRAME_AXES + ROW_AXES


def place(d):
    return d // 64, (d // 16) % 4, (d // 8) % 2, (d // 2) % 4, d % 2


def number(yh, z, yl, x, c):
    return ((yh * 4 + z) * 2 + yl) * 8 + x * 2 + c


def ring(axis):
    pairs = []
    for d in range(128):
        yh, z, yl, x, c = place(d)
        by = 1 - 2 * c
        if axis == "core":
            c = 1 - c
        elif axis == "x":
            x = (x + by) % 4
        elif axis == "z":
            z = (z + by) % 4
        else:
            y = (yh * 2 + yl + by) % 4
            yh, yl = y // 2, y % 2
        pairs.append((d, number(yh, z, yl, x, c)))
    return pairs


def moved(value, axis):
    return lax.ppermute(value, AXES, ring(axis))


def put(buf, part, *index):
    index = tuple(index) + (0,) * (buf.ndim - len(index))
    return lax.dynamic_update_slice(buf, part.reshape((1,) * (buf.ndim - part.ndim) + part.shape), index)


def take(value, index):
    return lax.dynamic_index_in_dim(value, index, 0, keepdims=False)


def gathered_axis(value, axis, mine, core):
    way = 1 - 2 * core
    full = moved(value, axis)
    half = moved(take(full, core), axis)
    other_full = moved(full, "core")
    other_half = moved(half, "core")
    buf = jnp.zeros((4,) + value.shape, value.dtype)
    buf = put(buf, value, mine)
    buf = put(buf, full, (mine - way) % 4)
    buf = put(buf, other_full, (mine + way) % 4)
    buf = put(buf, half, (mine + 2) % 4, core)
    return put(buf, other_half, (mine + 2) % 4, 1 - core)


def scattered_ring(own, send_half, keep_half, send_full, keep_full, axis, core):
    half = keep_half + moved(send_half, "core")
    passed = moved(half, axis)
    mine = (lax.broadcasted_iota(jnp.int32, (2, 1, 1), 0) == core)
    full = keep_full + moved(send_full, "core")
    full = (full + jnp.where(mine, passed[None], 0.0)).astype(BF16)
    return own + moved(full, axis).astype(F32)


def both_kernels(spatial, temporal, at):
    y, z, x, c = at
    chans = spatial.shape[1]
    rows_s, rows_t = spatial.shape[0], temporal.shape[0]
    own = jnp.concatenate([spatial, temporal], axis=0)
    other = moved(own, "core")
    pair = put(put(jnp.zeros((2,) + own.shape, own.dtype), own, c), other, 1 - c)
    rows = rows_s + rows_t
    units = gathered_axis(pair, "z", z, c)
    units = gathered_axis(units.reshape(2, 4 * rows, chans), "y", y, c)
    units = gathered_axis(units.reshape(2, 16 * rows, chans), "x", x, c)
    return units.reshape(4, 4, 4, 2 * rows, chans)


def unit_order(rows_s, rows_t):
    rows = rows_s + rows_t
    source = [rows * block + row for block in range(8) for row in range(rows_s)]
    source += [rows * block + rows_s + row for block in range(8) for row in range(rows_t)]
    return np.eye(8 * rows, dtype=np.float32)[source]


def summed_kernels(blocks, rows_s, rows_t, at):
    _, _, _, c = at
    chans = blocks[0].shape[-1]
    rows = 8 * (rows_s + rows_t)
    total = scattered_ring(*blocks, "y", c).reshape(4, rows, chans)
    total = jnp.concatenate(
        [
            total[:, : 8 * rows_s].reshape(4, 4, 2, rows_s, chans),
            total[:, 8 * rows_s :].reshape(4, 4, 2, rows_t, chans),
        ],
        axis=3,
    )
    keep = lax.dynamic_index_in_dim(total, c, 2, keepdims=False)
    send = lax.dynamic_index_in_dim(total, 1 - c, 2, keepdims=False)
    total = (keep + moved(send, "core")).reshape(16, rows_s + rows_t, chans)
    total = lax.all_to_all(total, ("z", "x"), split_axis=0, concat_axis=0, tiled=True)
    mine = jnp.sum(total, axis=0)
    return mine[:rows_s], mine[rows_s:]


def traded_edges(inner, outer):
    count = lax.axis_size(ROW_AXES)
    pairs = [(r, r + (1 if r % 2 else -1)) for r in range(count)]
    pairs = [(r, s) for r, s in pairs if 0 <= s < count]
    outer = lax.ppermute(outer, ROW_AXES, pairs)
    return moved(inner, "core"), outer


def edge_rows(value, core):
    last = value.shape[1] - 1
    inner = lax.dynamic_slice_in_dim(value, last * (1 - core), 1, 1)
    outer = lax.dynamic_slice_in_dim(value, last * core, 1, 1)
    return traded_edges(inner, outer)


def along_frames(value, by):
    count = lax.axis_size(FRAME_AXES)
    pairs = [(i, i + by) for i in range(count) if 0 <= i + by < count]
    return lax.ppermute(value, FRAME_AXES, pairs)


def sigmoid(value):
    return 1.0 / (1.0 + jnp.exp(-value))


def dot(left, right):
    return jnp.dot(left, right, preferred_element_type=F32)


def contract(left, right):
    return lax.dot_general(left, right, (((0,), (0,)), ((), ())), preferred_element_type=F32)


def normalize(cells):
    inv_rms = lax.rsqrt(jnp.mean(cells * cells, axis=-1, keepdims=True) + epsilon)
    return cells * inv_rms, inv_rms


def store_shifts(out, row, value):
    cols, chans = value.shape
    col = lax.broadcasted_iota(jnp.int32, value.shape, 0)
    before = jnp.where(col == 0, 0.0, pltpu.roll(value, 1, 0))
    after = jnp.where(col == cols - 1, 0.0, pltpu.roll(value, cols - 1, 0))
    out[row, :, :chans] = before.astype(BF16)
    out[row, :, chans : 2 * chans] = value.astype(BF16)
    out[row, :, 2 * chans :] = after.astype(BF16)


def halo_row(row, n_rows, core, inner, outer, body):
    if row == 0:
        return jnp.where(core == 0, outer[0, 0], inner[0, 0])
    if row > n_rows:
        return jnp.where(core == 0, inner[0, 0], outer[0, 0])
    return body[0, row - 1]


def activate_kernel(at, video, inner, outer, _, shifts):
    n_rows = video.shape[1]
    for row in range(n_rows + 2):
        cells = halo_row(row, n_rows, at[1], inner, outer, video)
        normed, _ = normalize(cells.astype(F32))
        store_shifts(shifts.at[0], row, normed * sigmoid(normed))


def unit_number(y, z):
    return ((y // 2) * 4 + z) * 2 + y % 2


def assemble_kernel(order, units, w_s, w_t, w_back):
    chans = w_s.shape[1]
    rows_s, rows_t = w_s.shape[0] // 16, w_t.shape[0] // 16
    for y in range(4):
        for z in range(4):
            u = unit_number(y, z)
            blocks = jnp.concatenate([units[x, y, z] for x in range(4)], axis=0)
            unit = dot(order[...], blocks).astype(BF16)
            w_s[rows_s * u : rows_s * (u + 1)] = unit[:rows_s]
            w_t[rows_t * u : rows_t * (u + 1)] = unit[rows_s:]
    for k in range(3):
        w_back[chans * k : chans * (k + 1)] = w_t[chans * (2 - k) : chans * (3 - k)].T


def reverse_kernel(w_s, w_rev):
    chans = w_s.shape[1]
    for k in range(9):
        w_rev[chans * k : chans * (k + 1)] = w_s[chans * (8 - k) : chans * (9 - k)].T


def cot_window(frame, cot0, cot1, cot2, ahead1, ahead2, rows, last):
    return (
        cot0[0, rows],
        jnp.where(frame >= last, ahead1[0, rows], cot1[0, rows]),
        jnp.where(frame >= last - 1, ahead2[0, rows], cot2[0, rows]),
    )


def forward_kernel(
    at, shifts, cot0, cot1, cot2, ahead1, ahead2, w_s, w_back, hidden, grad_pre, inner, outer
):
    _, n_rows, n_cols, chans = hidden.shape
    step, frame = 4, at[2] + pl.program_id(0)
    for row in range(0, n_rows, step):
        pre = None
        for tap in range(3):
            left = shifts[0, row + tap : row + tap + step].reshape(step * n_cols, 3 * chans)
            term = dot(left, w_s[3 * chans * tap : 3 * chans * (tap + 1)])
            pre = term if pre is None else pre + term
        back = None
        window = cot_window(
            frame, cot0, cot1, cot2, ahead1, ahead2, slice(row, row + step), at[3]
        )
        for k, cot in enumerate(window):
            left = cot.reshape(step * n_cols, chans)
            term = dot(left, w_back[chans * k : chans * (k + 1)])
            back = term if back is None else back + term
        gate = sigmoid(pre)
        hidden[0, row : row + step] = (pre * gate).astype(BF16).reshape(step, n_cols, chans)
        slope = gate * (1.0 + pre * (1.0 - gate))
        grad_pre[0, row : row + step] = (back * slope).astype(BF16).reshape(step, n_cols, chans)
    first, final = grad_pre[0, 0], grad_pre[0, n_rows - 1]
    inner[0, 0] = jnp.where(at[1] == 0, final, first)
    outer[0, 0] = jnp.where(at[1] == 0, first, final)


def weights_kernel(
    at, shifts, grad_pre, hidden, cot0, cot1, cot2, ahead1, ahead2,
    own, send_half, keep_half, send_full, keep_full, grad_s, grad_t,
):
    @pl.when(pl.program_id(0) == 0)
    def _():
        grad_s[...] = jnp.zeros_like(grad_s)
        grad_t[...] = jnp.zeros_like(grad_t)

    _, n_rows, n_cols, chans = hidden.shape
    cells = n_rows * n_cols
    last = pl.num_programs(0) - 1
    frame = pl.program_id(0)
    right = grad_pre[0].reshape(cells, chans)
    for tap in range(3):
        left = shifts[0, tap : tap + n_rows].reshape(cells, 3 * chans)
        grad_s[3 * chans * tap : 3 * chans * (tap + 1)] += contract(left, right)
    left = hidden[0].reshape(cells, chans)
    window = cot_window(frame, cot0, cot1, cot2, ahead1, ahead2, slice(0, n_rows), last)
    for k, cot in enumerate(window[::-1]):
        grad_t[chans * k : chans * (k + 1)] += contract(left, cot.reshape(cells, chans))

    @pl.when(pl.program_id(0) == last)
    def _():
        rows_s, rows_t = 9 * chans // 16, 3 * chans // 16
        mine, core = at[0], at[1]
        way = 1 - 2 * core

        def fill(out, index, y, z):
            u = unit_number(y, z)
            top = (index % 2) * (rows_s + rows_t)
            at_s = pl.ds(pl.multiple_of(rows_s * u, rows_t), rows_s)
            at_t = pl.ds(pl.multiple_of(rows_t * u, rows_t), rows_t)
            target = out if out.ndim == 2 else out.at[index // 2]
            target[top : top + rows_s] = grad_s[at_s]
            target[top + rows_s : top + rows_s + rows_t] = grad_t[at_t]

        for z in range(4):
            fill(own, z, mine, z)
            fill(send_full, z, lax.rem(mine + 4 - way, 4), z)
            fill(keep_full, z, lax.rem(mine + 4 + way, 4), z)
        opposite = lax.rem(mine + 2, 4)
        for z in range(2):
            fill(send_half, z, opposite, 2 * (1 - core) + z)
            fill(keep_half, z, opposite, 2 * core + z)


def backward_kernel(at, grad_pre, inner, outer, video, cot, w_rev, _, grad_video, shifts):
    _, n_rows, n_cols, chans = video.shape
    for row in range(n_rows + 2):
        cells = halo_row(row, n_rows, at[1], inner, outer, grad_pre)
        store_shifts(shifts, row, cells.astype(F32))
    step = 4
    for row in range(0, n_rows, step):
        grad_act = None
        for tap in range(3):
            left = shifts[row + tap : row + tap + step].reshape(step * n_cols, 3 * chans)
            term = dot(left, w_rev[3 * chans * tap : 3 * chans * (tap + 1)])
            grad_act = term if grad_act is None else grad_act + term
        cells = video[0, row : row + step].reshape(step * n_cols, chans).astype(F32)
        normed, inv_rms = normalize(cells)
        gate = sigmoid(normed)
        grad_norm = grad_act * (gate * (1.0 + normed * (1.0 - gate)))
        along = jnp.mean(grad_norm * normed, axis=-1, keepdims=True)
        grad_in = inv_rms * (grad_norm - normed * along)
        total = cot[0, row : row + step].reshape(step * n_cols, chans).astype(F32) + grad_in
        grad_video[0, row : row + step] = total.astype(BF16).reshape(step, n_cols, chans)


def output_kernel(at, video, past0, past1, hid0, hid1, hid2, w_t, _, output):
    frame = pl.program_id(0)
    _, n_rows, n_cols, chans = video.shape
    step = 4
    for row in range(0, n_rows, step):
        rows = slice(row, row + step)
        parts = (
            jnp.where(frame < 2, past0[0, rows], hid0[0, rows]),
            jnp.where(frame < 1, past1[0, rows], hid1[0, rows]),
            hid2[0, rows],
        )
        left = jnp.concatenate([part.reshape(step * n_cols, chans) for part in parts], axis=-1)
        cells = video[0, rows].reshape(step * n_cols, chans).astype(F32)
        mixed = dot(left, w_t[...])
        output[0, rows] = (cells + mixed).astype(BF16).reshape(step, n_cols, chans)


def frame_spec(shape, index=lambda f: f):
    return pl.BlockSpec((1,) + tuple(shape[1:]), lambda f, *_: (index(f), 0, 0, 0))


def whole(shape):
    return pl.BlockSpec(
        tuple(shape), lambda f, *_: (0,) * len(shape), pipeline_mode=pl.Buffered(1)
    )


def call(
    body, n_frames, in_specs, out_specs, out_shape, flops, scratch=(), scalars=0, aliases={},
    limit=20,
):
    return pl.pallas_call(
        body,
        grid_spec=pltpu.PrefetchScalarGridSpec(
            num_scalar_prefetch=scalars,
            grid=(n_frames,),
            in_specs=in_specs,
            out_specs=out_specs,
            scratch_shapes=scratch,
        ),
        out_shape=out_shape,
        input_output_aliases=aliases,
        cost_estimate=pl.CostEstimate(flops=flops, bytes_accessed=8 << 20, transcendentals=0),
        compiler_params=pltpu.CompilerParams(vmem_limit_bytes=limit << 20),
    )


def part_of(body, part, parts, specs, out, args, flops, scratch=(), before=None):
    count = out.shape[0] // parts
    base = part * count
    in_specs = []
    for shape, index in specs:
        if index is None:
            in_specs.append(whole(shape))
        else:
            in_specs.append(frame_spec(shape, lambda f, g=index: g(f, base)))
    if before is None:
        in_specs.append(pl.BlockSpec(memory_space=pltpu.SMEM))
        before, aliases = jnp.zeros((1,), jnp.int32), {}
    else:
        in_specs.append(pl.BlockSpec(memory_space=pl.ANY))
        aliases = {len(args): 0}
    return call(
        body,
        count,
        in_specs,
        frame_spec(out.shape, lambda f: f + base),
        out,
        flops // parts,
        scratch,
        1,
        aliases,
    )(*args, before)


def single(body, out_shapes, flops, *args, limit=12):
    return pl.pallas_call(
        body,
        in_specs=[pl.BlockSpec(memory_space=pltpu.VMEM)] * len(args),
        out_specs=[pl.BlockSpec(memory_space=pltpu.VMEM)] * len(out_shapes),
        out_shape=[jax.ShapeDtypeStruct(shape, BF16) for shape in out_shapes],
        cost_estimate=pl.CostEstimate(flops=flops, bytes_accessed=3 << 20, transcendentals=0),
        compiler_params=pltpu.CompilerParams(vmem_limit_bytes=limit << 20),
    )(*args)


def residual_block(video, spatial_weight, temporal_weight, cotangent):
    _, n_frames, n_rows, n_cols, chans = video.shape
    z, x, core = (lax.axis_index(axis) for axis in ("z", "x", "core"))
    y = lax.axis_index("y_hi") * 2 + lax.axis_index("y_lo")
    at = (y, z, x, core)
    video, cot = video[0], cotangent[0]
    shape = (n_frames, n_rows, n_cols, chans)
    wide = (n_frames, n_rows + 2, n_cols, 3 * chans)
    edge = (n_frames, 1, n_cols, chans)
    count = n_frames // 2
    half = (count,) + shape[1:]
    pair = 2 * n_frames * n_rows * n_cols * chans * chans
    rows_s, rows_t = spatial_weight.shape[0], temporal_weight.shape[0]
    rows = 8 * (rows_s + rows_t)
    last = n_frames - 1
    at_part = [jnp.stack([y, core, base, last]).astype(jnp.int32) for base in (0, count)]
    same = lambda f, base: f + base

    ahead = along_frames(cot[:2], -1)
    inner, outer = edge_rows(video, core)
    units = both_kernels(spatial_weight, temporal_weight, at)
    shifts = None
    for part in range(2):
        shifts = part_of(
            activate_kernel,
            part,
            2,
            [(shape, same), (edge, same), (edge, same)],
            jax.ShapeDtypeStruct(wide, BF16),
            (at_part[part], video, inner, outer),
            pair,
            before=shifts,
        )
    full_s, full_t = (9 * chans, chans), (3 * chans, chans)
    order = jnp.asarray(unit_order(rows_s, rows_t), BF16)
    w_s, w_t, w_back = single(assemble_kernel, (full_s, full_t, full_t), pair // 4, order, units)
    (w_rev,) = single(reverse_kernel, (full_s,), pair // 4, w_s)

    def cot_specs(base):
        specs = [
            frame_spec(shape, lambda f, k=k: jnp.minimum(f + base + k, last)) for k in range(3)
        ]
        return specs + [
            frame_spec(half, lambda f, k=k: jnp.maximum(f + base + k - last - 1, 0)) for k in (1, 2)
        ]

    hidden, grad_pre, edge_in, edge_out = call(
        forward_kernel,
        n_frames,
        [frame_spec(wide)] + cot_specs(0) + [whole(full_s), whole(full_t)],
        [frame_spec(shape)] * 2 + [frame_spec(edge)] * 2,
        [jax.ShapeDtypeStruct(shape, BF16)] * 2 + [jax.ShapeDtypeStruct(edge, BF16)] * 2,
        12 * pair,
        scalars=1,
    )(at_part[0], shifts, cot, cot, cot, ahead, ahead, w_s, w_back)
    edges = traded_edges(edge_in, edge_out)
    past = along_frames(hidden[count:], 1)
    block, half_block = (2, 2 * rows, chans), (2 * rows, chans)
    block_shapes = (block, half_block, half_block, block, block)
    blocks = call(
        weights_kernel,
        n_frames,
        [frame_spec(wide), frame_spec(shape), frame_spec(shape)] + cot_specs(0),
        [whole(shape_) for shape_ in block_shapes],
        [jax.ShapeDtypeStruct(shape_, F32) for shape_ in block_shapes],
        12 * pair,
        [pltpu.VMEM(full_s, F32), pltpu.VMEM(full_t, F32)],
        scalars=1,
        limit=28,
    )(at_part[0], shifts, grad_pre, hidden, cot, cot, cot, ahead, ahead)
    grad_video = part_of(
        backward_kernel,
        0,
        1,
        [(shape, same), (edge, same), (edge, same), (shape, same), (shape, same), (full_s, None)],
        jax.ShapeDtypeStruct(shape, BF16),
        (at_part[0], grad_pre, *edges, video, cot, w_rev),
        9 * pair,
        [pltpu.VMEM(wide[1:], BF16)],
    )
    output = part_of(
        output_kernel,
        0,
        1,
        [
            (shape, same),
            (half, lambda f, base: jnp.minimum(f, count - 1)),
            (half, lambda f, base: count - 1),
            (shape, lambda f, base: jnp.maximum(f - 2, 0)),
            (shape, lambda f, base: jnp.maximum(f - 1, 0)),
            (shape, same),
            (full_t, None),
        ],
        jax.ShapeDtypeStruct(shape, BF16),
        (at_part[0], video, past, past, hidden, hidden, hidden, w_t),
        3 * pair,
    )
    spatial_part, temporal_part = summed_kernels(blocks, rows_s, rows_t, at)
    total_cells = n_frames * n_rows * n_cols * lax.axis_size(AXES)
    factor = float(total_cells) ** (-0.5)
    return (output[None], grad_video[None], spatial_part * factor, temporal_part * factor)


def solution(mesh):
    fine = Mesh(mesh.devices.reshape(2, 4, 2, 4, 2), AXES)
    cells = P(None, FRAME_AXES, ROW_AXES, None, None)
    kernels = P(AXES, None)
    return jax.shard_map(
        residual_block,
        mesh=fine,
        in_specs=(cells, kernels, kernels, cells),
        out_specs=(cells, cells, kernels, kernels),
        check_vma=False,
    )
```

```python
import jax
import jax.numpy as jnp
import numpy as np
from jax import lax
from jax.experimental import pallas as pl
from jax.experimental.pallas import tpu as pltpu
from jax.sharding import Mesh
from jax.sharding import PartitionSpec as P


epsilon = 1e-06
F32, BF16 = jnp.float32, jnp.bfloat16
FRAME_AXES, ROW_AXES = ("y_hi", "z"), ("y_lo", "x", "core")
AXES = FRAME_AXES + ROW_AXES
UNIT_AXES = ("y_hi", "z", "y_lo")


def place(d):
    return d // 64, (d // 16) % 4, (d // 8) % 2, (d // 2) % 4, d % 2


def number(yh, z, yl, x, c):
    return ((yh * 4 + z) * 2 + yl) * 8 + x * 2 + c


def ring(axis):
    pairs = []
    for d in range(128):
        yh, z, yl, x, c = place(d)
        by = 1 - 2 * c
        if axis == "core":
            c = 1 - c
        elif axis == "x":
            x = (x + by) % 4
        elif axis == "z":
            z = (z + by) % 4
        else:
            y = (yh * 2 + yl + by) % 4
            yh, yl = y // 2, y % 2
        pairs.append((d, number(yh, z, yl, x, c)))
    return pairs


def moved(value, axis):
    return lax.ppermute(value, AXES, ring(axis))


def put(buf, part, *index):
    index = tuple(index) + (0,) * (buf.ndim - len(index))
    return lax.dynamic_update_slice(buf, part.reshape((1,) * (buf.ndim - part.ndim) + part.shape), index)


def take(value, index):
    return lax.dynamic_index_in_dim(value, index, 0, keepdims=False)


def gathered_axis(value, axis, mine, core):
    way = 1 - 2 * core
    full = moved(value, axis)
    half = moved(take(full, core), axis)
    other_full = moved(full, "core")
    other_half = moved(half, "core")
    buf = jnp.zeros((4,) + value.shape, value.dtype)
    buf = put(buf, value, mine)
    buf = put(buf, full, (mine - way) % 4)
    buf = put(buf, other_full, (mine + way) % 4)
    buf = put(buf, half, (mine + 2) % 4, core)
    return put(buf, other_half, (mine + 2) % 4, 1 - core)


def scattered_ring(own, send_half, keep_half, send_full, keep_full, axis, core):
    half = keep_half + moved(send_half, "core")
    passed = moved(half, axis)
    mine = (lax.broadcasted_iota(jnp.int32, (2, 1, 1), 0) == core)
    full = keep_full + moved(send_full, "core")
    full = (full + jnp.where(mine, passed[None], 0.0)).astype(BF16)
    return own + moved(full, axis).astype(F32)


def both_kernels(spatial, temporal, at):
    x, c = at
    own = jnp.concatenate([spatial, temporal], axis=0)
    rows, chans = own.shape
    copies = jnp.broadcast_to(own[None], (16, rows, chans))
    units = lax.all_to_all(copies, UNIT_AXES, split_axis=0, concat_axis=0, tiled=True)
    units = units.reshape(16 * rows, chans)
    other = moved(units, "core")
    pair = put(put(jnp.zeros((2, 16 * rows, chans), units.dtype), units, c), other, 1 - c)
    return gathered_axis(pair, "x", x, c).reshape(4, 2, 16, rows, chans)


def unit_order(rows_s, rows_t):
    rows = rows_s + rows_t
    source = [rows * block + row for block in range(8) for row in range(rows_s)]
    source += [rows * block + rows_s + row for block in range(8) for row in range(rows_t)]
    return np.eye(8 * rows, dtype=np.float32)[source]


def summed_kernels(blocks, rows_s, rows_t, core):
    chans = blocks[0].shape[-1]
    total = scattered_ring(*blocks, "x", core).reshape(16, 2, rows_s + rows_t, chans)
    keep = lax.dynamic_index_in_dim(total, core, 1, keepdims=False)
    send = lax.dynamic_index_in_dim(total, 1 - core, 1, keepdims=False)
    total = keep + moved(send, "core")
    total = lax.all_to_all(total, UNIT_AXES, split_axis=0, concat_axis=0, tiled=True)
    mine = jnp.sum(total, axis=0)
    return mine[:rows_s], mine[rows_s:]


def traded_edges(inner, outer):
    count = lax.axis_size(ROW_AXES)
    pairs = [(r, r + (1 if r % 2 else -1)) for r in range(count)]
    pairs = [(r, s) for r, s in pairs if 0 <= s < count]
    outer = lax.ppermute(outer, ROW_AXES, pairs)
    return moved(inner, "core"), outer


def edge_rows(value, core):
    last = value.shape[1] - 1
    inner = lax.dynamic_slice_in_dim(value, last * (1 - core), 1, 1)
    outer = lax.dynamic_slice_in_dim(value, last * core, 1, 1)
    return traded_edges(inner, outer)


def along_frames(value, by):
    count = lax.axis_size(FRAME_AXES)
    pairs = [(i, i + by) for i in range(count) if 0 <= i + by < count]
    return lax.ppermute(value, FRAME_AXES, pairs)


def sigmoid(value):
    return 1.0 / (1.0 + jnp.exp(-value))


def dot(left, right):
    return jnp.dot(left, right, preferred_element_type=F32)


def contract(left, right):
    return lax.dot_general(left, right, (((0,), (0,)), ((), ())), preferred_element_type=F32)


def normalize(cells):
    inv_rms = lax.rsqrt(jnp.mean(cells * cells, axis=-1, keepdims=True) + epsilon)
    return cells * inv_rms, inv_rms


def store_shifts(out, row, value):
    cols, chans = value.shape
    col = lax.broadcasted_iota(jnp.int32, value.shape, 0)
    before = jnp.where(col == 0, 0.0, pltpu.roll(value, 1, 0))
    after = jnp.where(col == cols - 1, 0.0, pltpu.roll(value, cols - 1, 0))
    out[row, :, :chans] = before.astype(BF16)
    out[row, :, chans : 2 * chans] = value.astype(BF16)
    out[row, :, 2 * chans :] = after.astype(BF16)


def halo_row(row, n_rows, core, inner, outer, body):
    if row == 0:
        return jnp.where(core == 0, outer[0, 0], inner[0, 0])
    if row > n_rows:
        return jnp.where(core == 0, inner[0, 0], outer[0, 0])
    return body[0, row - 1]


def activate_kernel(at, video, inner, outer, _, shifts):
    n_rows = video.shape[1]
    for row in range(n_rows + 2):
        cells = halo_row(row, n_rows, at[1], inner, outer, video)
        normed, _ = normalize(cells.astype(F32))
        store_shifts(shifts.at[0], row, normed * sigmoid(normed))


def assemble_kernel(order, units, w_s, w_t, w_back):
    chans = w_s.shape[1]
    rows_s, rows_t = w_s.shape[0] // 16, w_t.shape[0] // 16
    for u in range(16):
        blocks = [units[x, core, u] for x in range(4) for core in range(2)]
        unit = dot(order[...], jnp.concatenate(blocks, axis=0)).astype(BF16)
        w_s[rows_s * u : rows_s * (u + 1)] = unit[:rows_s]
        w_t[rows_t * u : rows_t * (u + 1)] = unit[rows_s:]
    for k in range(3):
        w_back[chans * k : chans * (k + 1)] = w_t[chans * (2 - k) : chans * (3 - k)].T


def reverse_kernel(w_s, w_rev):
    chans = w_s.shape[1]
    for k in range(9):
        w_rev[chans * k : chans * (k + 1)] = w_s[chans * (8 - k) : chans * (9 - k)].T


def cot_window(frame, cot0, cot1, cot2, ahead1, ahead2, rows, last):
    return (
        cot0[0, rows],
        jnp.where(frame >= last, ahead1[0, rows], cot1[0, rows]),
        jnp.where(frame >= last - 1, ahead2[0, rows], cot2[0, rows]),
    )


def forward_kernel(
    at, shifts, cot0, cot1, cot2, ahead1, ahead2, w_s, w_back, hidden, grad_pre, inner, outer
):
    _, n_rows, n_cols, chans = hidden.shape
    step, frame = 4, at[2] + pl.program_id(0)
    for row in range(0, n_rows, step):
        pre = None
        for tap in range(3):
            left = shifts[0, row + tap : row + tap + step].reshape(step * n_cols, 3 * chans)
            term = dot(left, w_s[3 * chans * tap : 3 * chans * (tap + 1)])
            pre = term if pre is None else pre + term
        back = None
        window = cot_window(
            frame, cot0, cot1, cot2, ahead1, ahead2, slice(row, row + step), at[3]
        )
        for k, cot in enumerate(window):
            left = cot.reshape(step * n_cols, chans)
            term = dot(left, w_back[chans * k : chans * (k + 1)])
            back = term if back is None else back + term
        gate = sigmoid(pre)
        hidden[0, row : row + step] = (pre * gate).astype(BF16).reshape(step, n_cols, chans)
        slope = gate * (1.0 + pre * (1.0 - gate))
        grad_pre[0, row : row + step] = (back * slope).astype(BF16).reshape(step, n_cols, chans)
    first, final = grad_pre[0, 0], grad_pre[0, n_rows - 1]
    inner[0, 0] = jnp.where(at[1] == 0, final, first)
    outer[0, 0] = jnp.where(at[1] == 0, first, final)


def weights_kernel(
    at, shifts, grad_pre, hidden, cot0, cot1, cot2, ahead1, ahead2,
    own, send_half, keep_half, send_full, keep_full, grad_s, grad_t, by_x,
):
    @pl.when(pl.program_id(0) == 0)
    def _():
        grad_s[...] = jnp.zeros_like(grad_s)
        grad_t[...] = jnp.zeros_like(grad_t)

    _, n_rows, n_cols, chans = hidden.shape
    cells = n_rows * n_cols
    last = pl.num_programs(0) - 1
    frame = pl.program_id(0)
    right = grad_pre[0].reshape(cells, chans)
    for tap in range(3):
        left = shifts[0, tap : tap + n_rows].reshape(cells, 3 * chans)
        grad_s[3 * chans * tap : 3 * chans * (tap + 1)] += contract(left, right)
    left = hidden[0].reshape(cells, chans)
    window = cot_window(frame, cot0, cot1, cot2, ahead1, ahead2, slice(0, n_rows), last)
    for k, cot in enumerate(window[::-1]):
        grad_t[chans * k : chans * (k + 1)] += contract(left, cot.reshape(cells, chans))

    @pl.when(pl.program_id(0) == last)
    def _():
        rows_s, rows_t = 9 * chans // 128, 3 * chans // 128
        rows = rows_s + rows_t
        for u in range(16):
            for block in range(8):
                x, row, number = block // 2, (2 * u + block % 2) * rows, 8 * u + block
                by_x[x, row : row + rows] = jnp.concatenate(
                    [
                        grad_s[rows_s * number : rows_s * (number + 1)],
                        grad_t[rows_t * number : rows_t * (number + 1)],
                    ],
                    axis=0,
                )
        mine, core = at[0], at[1]
        way = 1 - 2 * core
        half = 16 * rows
        own[...] = by_x[mine].reshape(own.shape)
        send_full[...] = by_x[lax.rem(mine + 4 - way, 4)].reshape(own.shape)
        keep_full[...] = by_x[lax.rem(mine + 4 + way, 4)].reshape(own.shape)
        opposite = lax.rem(mine + 2, 4)
        send_half[...] = by_x[opposite, pl.ds(pl.multiple_of((1 - core) * half, half), half)]
        keep_half[...] = by_x[opposite, pl.ds(pl.multiple_of(core * half, half), half)]


def backward_kernel(at, grad_pre, inner, outer, video, cot, w_rev, _, grad_video, shifts):
    _, n_rows, n_cols, chans = video.shape
    for row in range(n_rows + 2):
        cells = halo_row(row, n_rows, at[1], inner, outer, grad_pre)
        store_shifts(shifts, row, cells.astype(F32))
    step = 4
    for row in range(0, n_rows, step):
        grad_act = None
        for tap in range(3):
            left = shifts[row + tap : row + tap + step].reshape(step * n_cols, 3 * chans)
            term = dot(left, w_rev[3 * chans * tap : 3 * chans * (tap + 1)])
            grad_act = term if grad_act is None else grad_act + term
        cells = video[0, row : row + step].reshape(step * n_cols, chans).astype(F32)
        normed, inv_rms = normalize(cells)
        gate = sigmoid(normed)
        grad_norm = grad_act * (gate * (1.0 + normed * (1.0 - gate)))
        along = jnp.mean(grad_norm * normed, axis=-1, keepdims=True)
        grad_in = inv_rms * (grad_norm - normed * along)
        total = cot[0, row : row + step].reshape(step * n_cols, chans).astype(F32) + grad_in
        grad_video[0, row : row + step] = total.astype(BF16).reshape(step, n_cols, chans)


def output_kernel(at, video, past0, past1, hid0, hid1, hid2, w_t, _, output):
    frame = pl.program_id(0)
    _, n_rows, n_cols, chans = video.shape
    step = 4
    for row in range(0, n_rows, step):
        rows = slice(row, row + step)
        parts = (
            jnp.where(frame < 2, past0[0, rows], hid0[0, rows]),
            jnp.where(frame < 1, past1[0, rows], hid1[0, rows]),
            hid2[0, rows],
        )
        left = jnp.concatenate([part.reshape(step * n_cols, chans) for part in parts], axis=-1)
        cells = video[0, rows].reshape(step * n_cols, chans).astype(F32)
        mixed = dot(left, w_t[...])
        output[0, rows] = (cells + mixed).astype(BF16).reshape(step, n_cols, chans)


def frame_spec(shape, index=lambda f: f):
    return pl.BlockSpec((1,) + tuple(shape[1:]), lambda f, *_: (index(f), 0, 0, 0))


def whole(shape):
    return pl.BlockSpec(
        tuple(shape), lambda f, *_: (0,) * len(shape), pipeline_mode=pl.Buffered(1)
    )


def call(
    body, n_frames, in_specs, out_specs, out_shape, flops, scratch=(), scalars=0, aliases={},
    limit=20,
):
    return pl.pallas_call(
        body,
        grid_spec=pltpu.PrefetchScalarGridSpec(
            num_scalar_prefetch=scalars,
            grid=(n_frames,),
            in_specs=in_specs,
            out_specs=out_specs,
            scratch_shapes=scratch,
        ),
        out_shape=out_shape,
        input_output_aliases=aliases,
        cost_estimate=pl.CostEstimate(flops=flops, bytes_accessed=8 << 20, transcendentals=0),
        compiler_params=pltpu.CompilerParams(vmem_limit_bytes=limit << 20),
    )


def part_of(body, part, parts, specs, out, args, flops, scratch=(), before=None):
    count = out.shape[0] // parts
    base = part * count
    in_specs = []
    for shape, index in specs:
        if index is None:
            in_specs.append(whole(shape))
        else:
            in_specs.append(frame_spec(shape, lambda f, g=index: g(f, base)))
    if before is None:
        in_specs.append(pl.BlockSpec(memory_space=pltpu.SMEM))
        before, aliases = jnp.zeros((1,), jnp.int32), {}
    else:
        in_specs.append(pl.BlockSpec(memory_space=pl.ANY))
        aliases = {len(args): 0}
    return call(
        body,
        count,
        in_specs,
        frame_spec(out.shape, lambda f: f + base),
        out,
        flops // parts,
        scratch,
        1,
        aliases,
    )(*args, before)


def single(body, out_shapes, flops, *args, limit=12):
    return pl.pallas_call(
        body,
        in_specs=[pl.BlockSpec(memory_space=pltpu.VMEM)] * len(args),
        out_specs=[pl.BlockSpec(memory_space=pltpu.VMEM)] * len(out_shapes),
        out_shape=[jax.ShapeDtypeStruct(shape, BF16) for shape in out_shapes],
        cost_estimate=pl.CostEstimate(flops=flops, bytes_accessed=3 << 20, transcendentals=0),
        compiler_params=pltpu.CompilerParams(vmem_limit_bytes=limit << 20),
    )(*args)


def residual_block(video, spatial_weight, temporal_weight, cotangent):
    _, n_frames, n_rows, n_cols, chans = video.shape
    x, core = lax.axis_index("x"), lax.axis_index("core")
    video, cot = video[0], cotangent[0]
    shape = (n_frames, n_rows, n_cols, chans)
    wide = (n_frames, n_rows + 2, n_cols, 3 * chans)
    edge = (n_frames, 1, n_cols, chans)
    count = n_frames // 2
    half = (count,) + shape[1:]
    pair = 2 * n_frames * n_rows * n_cols * chans * chans
    rows_s, rows_t = spatial_weight.shape[0], temporal_weight.shape[0]
    rows = 8 * (rows_s + rows_t)
    last = n_frames - 1
    at_part = [jnp.stack([x, core, base, last]).astype(jnp.int32) for base in (0, count)]
    same = lambda f, base: f + base

    ahead = along_frames(cot[:2], -1)
    inner, outer = edge_rows(video, core)
    units = both_kernels(spatial_weight, temporal_weight, (x, core))
    shifts = None
    for part in range(2):
        shifts = part_of(
            activate_kernel,
            part,
            2,
            [(shape, same), (edge, same), (edge, same)],
            jax.ShapeDtypeStruct(wide, BF16),
            (at_part[part], video, inner, outer),
            pair,
            before=shifts,
        )
    full_s, full_t = (9 * chans, chans), (3 * chans, chans)
    order = jnp.asarray(unit_order(rows_s, rows_t), BF16)
    w_s, w_t, w_back = single(assemble_kernel, (full_s, full_t, full_t), pair // 4, order, units)
    (w_rev,) = single(reverse_kernel, (full_s,), pair // 4, w_s)

    def cot_specs(base):
        specs = [
            frame_spec(shape, lambda f, k=k: jnp.minimum(f + base + k, last)) for k in range(3)
        ]
        return specs + [
            frame_spec(half, lambda f, k=k: jnp.maximum(f + base + k - last - 1, 0)) for k in (1, 2)
        ]

    hidden, grad_pre, edge_in, edge_out = call(
        forward_kernel,
        n_frames,
        [frame_spec(wide)] + cot_specs(0) + [whole(full_s), whole(full_t)],
        [frame_spec(shape)] * 2 + [frame_spec(edge)] * 2,
        [jax.ShapeDtypeStruct(shape, BF16)] * 2 + [jax.ShapeDtypeStruct(edge, BF16)] * 2,
        12 * pair,
        scalars=1,
    )(at_part[0], shifts, cot, cot, cot, ahead, ahead, w_s, w_back)
    edges = traded_edges(edge_in, edge_out)
    past = along_frames(hidden[count:], 1)
    block, half_block = (2, 2 * rows, chans), (2 * rows, chans)
    block_shapes = (block, half_block, half_block, block, block)
    blocks = call(
        weights_kernel,
        n_frames,
        [frame_spec(wide), frame_spec(shape), frame_spec(shape)] + cot_specs(0),
        [whole(shape_) for shape_ in block_shapes],
        [jax.ShapeDtypeStruct(shape_, F32) for shape_ in block_shapes],
        12 * pair,
        [pltpu.VMEM(full_s, F32), pltpu.VMEM(full_t, F32), pltpu.VMEM((4, 4 * rows, chans), F32)],
        scalars=1,
        limit=32,
    )(at_part[0], shifts, grad_pre, hidden, cot, cot, cot, ahead, ahead)
    grad_video = part_of(
        backward_kernel,
        0,
        1,
        [(shape, same), (edge, same), (edge, same), (shape, same), (shape, same), (full_s, None)],
        jax.ShapeDtypeStruct(shape, BF16),
        (at_part[0], grad_pre, *edges, video, cot, w_rev),
        9 * pair,
        [pltpu.VMEM(wide[1:], BF16)],
    )
    output = part_of(
        output_kernel,
        0,
        1,
        [
            (shape, same),
            (half, lambda f, base: jnp.minimum(f, count - 1)),
            (half, lambda f, base: count - 1),
            (shape, lambda f, base: jnp.maximum(f - 2, 0)),
            (shape, lambda f, base: jnp.maximum(f - 1, 0)),
            (shape, same),
            (full_t, None),
        ],
        jax.ShapeDtypeStruct(shape, BF16),
        (at_part[0], video, past, past, hidden, hidden, hidden, w_t),
        3 * pair,
    )
    spatial_part, temporal_part = summed_kernels(blocks, rows_s, rows_t, core)
    total_cells = n_frames * n_rows * n_cols * lax.axis_size(AXES)
    factor = float(total_cells) ** (-0.5)
    return (output[None], grad_video[None], spatial_part * factor, temporal_part * factor)


def solution(mesh):
    fine = Mesh(mesh.devices.reshape(2, 4, 2, 4, 2), AXES)
    cells = P(None, FRAME_AXES, ROW_AXES, None, None)
    kernels = P(AXES, None)
    return jax.shard_map(
        residual_block,
        mesh=fine,
        in_specs=(cells, kernels, kernels, cells),
        out_specs=(cells, cells, kernels, kernels),
        check_vma=False,
    )
```

```python
import jax
import jax.numpy as jnp
import numpy as np
from jax import lax
from jax.experimental import pallas as pl
from jax.experimental.pallas import tpu as pltpu
from jax.sharding import Mesh
from jax.sharding import PartitionSpec as P


epsilon = 1e-06
F32, BF16 = jnp.float32, jnp.bfloat16
FRAME_AXES, ROW_AXES = ("y_hi", "z"), ("y_lo", "x", "core")
AXES = FRAME_AXES + ROW_AXES
UNIT_AXES = ("y_hi", "z", "y_lo")


def place(d):
    return d // 64, (d // 16) % 4, (d // 8) % 2, (d // 2) % 4, d % 2


def number(yh, z, yl, x, c):
    return ((yh * 4 + z) * 2 + yl) * 8 + x * 2 + c


def ring(axis):
    pairs = []
    for d in range(128):
        yh, z, yl, x, c = place(d)
        by = 1 - 2 * c
        if axis == "core":
            c = 1 - c
        elif axis == "x":
            x = (x + by) % 4
        elif axis == "z":
            z = (z + by) % 4
        else:
            y = (yh * 2 + yl + by) % 4
            yh, yl = y // 2, y % 2
        pairs.append((d, number(yh, z, yl, x, c)))
    return pairs


def moved(value, axis):
    return lax.ppermute(value, AXES, ring(axis))


def put(buf, part, *index):
    index = tuple(index) + (0,) * (buf.ndim - len(index))
    return lax.dynamic_update_slice(buf, part.reshape((1,) * (buf.ndim - part.ndim) + part.shape), index)


def take(value, index):
    return lax.dynamic_index_in_dim(value, index, 0, keepdims=False)


def gathered_axis(value, axis, mine, core):
    way = 1 - 2 * core
    full = moved(value, axis)
    half = moved(take(full, core), axis)
    other_full = moved(full, "core")
    other_half = moved(half, "core")
    buf = jnp.zeros((4,) + value.shape, value.dtype)
    buf = put(buf, value, mine)
    buf = put(buf, full, (mine - way) % 4)
    buf = put(buf, other_full, (mine + way) % 4)
    buf = put(buf, half, (mine + 2) % 4, core)
    return put(buf, other_half, (mine + 2) % 4, 1 - core)


def scattered_ring(own, send_half, keep_half, send_full, keep_full, axis, core):
    half = keep_half + moved(send_half, "core")
    passed = moved(half, axis)
    mine = (lax.broadcasted_iota(jnp.int32, (2, 1, 1), 0) == core)
    full = keep_full + moved(send_full, "core")
    full = (full + jnp.where(mine, passed[None], 0.0)).astype(BF16)
    return own + moved(full, axis).astype(F32)


def both_kernels(spatial, temporal, at):
    x, c = at
    own = jnp.concatenate([spatial, temporal], axis=0)
    rows, chans = own.shape
    copies = jnp.broadcast_to(own[None], (16, rows, chans))
    units = lax.all_to_all(copies, UNIT_AXES, split_axis=0, concat_axis=0, tiled=True)
    units = units.reshape(16 * rows, chans)
    other = moved(units, "core")
    pair = put(put(jnp.zeros((2, 16 * rows, chans), units.dtype), units, c), other, 1 - c)
    return gathered_axis(pair, "x", x, c).reshape(4, 2, 16, rows, chans)


def unit_order(rows_s, rows_t):
    rows = rows_s + rows_t
    source = [rows * block + row for block in range(8) for row in range(rows_s)]
    source += [rows * block + rows_s + row for block in range(8) for row in range(rows_t)]
    return np.eye(8 * rows, dtype=np.float32)[source]


def summed_kernels(blocks, rows_s, rows_t, core):
    chans = blocks[0].shape[-1]
    total = scattered_ring(*blocks, "x", core).reshape(16, 2, rows_s + rows_t, chans)
    keep = lax.dynamic_index_in_dim(total, core, 1, keepdims=False)
    send = lax.dynamic_index_in_dim(total, 1 - core, 1, keepdims=False)
    total = keep + moved(send, "core")
    total = lax.all_to_all(total, UNIT_AXES, split_axis=0, concat_axis=0, tiled=True)
    mine = jnp.sum(total, axis=0)
    return mine[:rows_s], mine[rows_s:]


def traded_edges(inner, outer):
    count = lax.axis_size(ROW_AXES)
    pairs = [(r, r + (1 if r % 2 else -1)) for r in range(count)]
    pairs = [(r, s) for r, s in pairs if 0 <= s < count]
    outer = lax.ppermute(outer, ROW_AXES, pairs)
    return moved(inner, "core"), outer


def edge_rows(value, core):
    last = value.shape[1] - 1
    inner = lax.dynamic_slice_in_dim(value, last * (1 - core), 1, 1)
    outer = lax.dynamic_slice_in_dim(value, last * core, 1, 1)
    return traded_edges(inner, outer)


def along_frames(value, by):
    count = lax.axis_size(FRAME_AXES)
    pairs = [(i, i + by) for i in range(count) if 0 <= i + by < count]
    return lax.ppermute(value, FRAME_AXES, pairs)


def sigmoid(value):
    return 1.0 / (1.0 + jnp.exp(-value))


def dot(left, right):
    return jnp.dot(left, right, preferred_element_type=F32)


def contract(left, right):
    return lax.dot_general(left, right, (((0,), (0,)), ((), ())), preferred_element_type=F32)


def normalize(cells):
    inv_rms = lax.rsqrt(jnp.mean(cells * cells, axis=-1, keepdims=True) + epsilon)
    return cells * inv_rms, inv_rms


def store_shifts(out, row, value):
    cols, chans = value.shape
    col = lax.broadcasted_iota(jnp.int32, value.shape, 0)
    before = jnp.where(col == 0, 0.0, pltpu.roll(value, 1, 0))
    after = jnp.where(col == cols - 1, 0.0, pltpu.roll(value, cols - 1, 0))
    out[row, :, :chans] = before.astype(BF16)
    out[row, :, chans : 2 * chans] = value.astype(BF16)
    out[row, :, 2 * chans :] = after.astype(BF16)


def halo_row(row, n_rows, core, inner, outer, body):
    if row == 0:
        return jnp.where(core == 0, outer[0, 0], inner[0, 0])
    if row > n_rows:
        return jnp.where(core == 0, inner[0, 0], outer[0, 0])
    return body[0, row - 1]


def activate_kernel(at, video, inner, outer, _, shifts):
    n_rows = video.shape[1]
    for row in range(n_rows + 2):
        cells = halo_row(row, n_rows, at[1], inner, outer, video)
        normed, _ = normalize(cells.astype(F32))
        store_shifts(shifts.at[0], row, normed * sigmoid(normed))


def assemble_kernel(order, units, w_s, w_t, w_back):
    chans = w_s.shape[1]
    rows_s, rows_t = w_s.shape[0] // 16, w_t.shape[0] // 16
    for u in range(16):
        blocks = [units[x, core, u] for x in range(4) for core in range(2)]
        unit = dot(order[...], jnp.concatenate(blocks, axis=0)).astype(BF16)
        w_s[rows_s * u : rows_s * (u + 1)] = unit[:rows_s]
        w_t[rows_t * u : rows_t * (u + 1)] = unit[rows_s:]
    for k in range(3):
        w_back[chans * k : chans * (k + 1)] = w_t[chans * (2 - k) : chans * (3 - k)].T


def reverse_kernel(w_s, w_rev):
    chans = w_s.shape[1]
    for k in range(9):
        w_rev[chans * k : chans * (k + 1)] = w_s[chans * (8 - k) : chans * (9 - k)].T


def cot_window(frame, cot0, cot1, cot2, ahead1, ahead2, rows, last):
    return (
        cot0[0, rows],
        jnp.where(frame >= last, ahead1[0, rows], cot1[0, rows]),
        jnp.where(frame >= last - 1, ahead2[0, rows], cot2[0, rows]),
    )


def forward_kernel(
    at, shifts, cot0, cot1, cot2, ahead1, ahead2, w_s, w_back, *outputs
):
    hidden, grad_pre, inner, outer = outputs[-4:]
    _, n_rows, n_cols, chans = hidden.shape
    step, frame = 4, at[2] + pl.program_id(0)
    for row in range(0, n_rows, step):
        pre = None
        for tap in range(3):
            left = shifts[0, row + tap : row + tap + step].reshape(step * n_cols, 3 * chans)
            term = dot(left, w_s[3 * chans * tap : 3 * chans * (tap + 1)])
            pre = term if pre is None else pre + term
        back = None
        window = cot_window(
            frame, cot0, cot1, cot2, ahead1, ahead2, slice(row, row + step), at[3]
        )
        for k, cot in enumerate(window):
            left = cot.reshape(step * n_cols, chans)
            term = dot(left, w_back[chans * k : chans * (k + 1)])
            back = term if back is None else back + term
        gate = sigmoid(pre)
        hidden[0, row : row + step] = (pre * gate).astype(BF16).reshape(step, n_cols, chans)
        slope = gate * (1.0 + pre * (1.0 - gate))
        grad_pre[0, row : row + step] = (back * slope).astype(BF16).reshape(step, n_cols, chans)
    first, final = grad_pre[0, 0], grad_pre[0, n_rows - 1]
    inner[0, 0] = jnp.where(at[1] == 0, final, first)
    outer[0, 0] = jnp.where(at[1] == 0, first, final)


def weights_kernel(
    at, shifts, grad_pre, hidden, cot0, cot1, cot2, ahead1, ahead2,
    own, send_half, keep_half, send_full, keep_full, grad_s, grad_t, by_x,
):
    @pl.when(pl.program_id(0) == 0)
    def _():
        grad_s[...] = jnp.zeros_like(grad_s)
        grad_t[...] = jnp.zeros_like(grad_t)

    _, n_rows, n_cols, chans = hidden.shape
    cells = n_rows * n_cols
    last = pl.num_programs(0) - 1
    frame = pl.program_id(0)
    right = grad_pre[0].reshape(cells, chans)
    for tap in range(3):
        left = shifts[0, tap : tap + n_rows].reshape(cells, 3 * chans)
        grad_s[3 * chans * tap : 3 * chans * (tap + 1)] += contract(left, right)
    left = hidden[0].reshape(cells, chans)
    window = cot_window(frame, cot0, cot1, cot2, ahead1, ahead2, slice(0, n_rows), last)
    for k, cot in enumerate(window[::-1]):
        grad_t[chans * k : chans * (k + 1)] += contract(left, cot.reshape(cells, chans))

    @pl.when(pl.program_id(0) == last)
    def _():
        rows_s, rows_t = 9 * chans // 128, 3 * chans // 128
        rows = rows_s + rows_t
        for u in range(16):
            for block in range(8):
                x, row, number = block // 2, (2 * u + block % 2) * rows, 8 * u + block
                by_x[x, row : row + rows] = jnp.concatenate(
                    [
                        grad_s[rows_s * number : rows_s * (number + 1)],
                        grad_t[rows_t * number : rows_t * (number + 1)],
                    ],
                    axis=0,
                )
        mine, core = at[0], at[1]
        way = 1 - 2 * core
        half = 16 * rows
        own[...] = by_x[mine].reshape(own.shape)
        send_full[...] = by_x[lax.rem(mine + 4 - way, 4)].reshape(own.shape)
        keep_full[...] = by_x[lax.rem(mine + 4 + way, 4)].reshape(own.shape)
        opposite = lax.rem(mine + 2, 4)
        send_half[...] = by_x[opposite, pl.ds(pl.multiple_of((1 - core) * half, half), half)]
        keep_half[...] = by_x[opposite, pl.ds(pl.multiple_of(core * half, half), half)]


def backward_kernel(at, grad_pre, inner, outer, video, cot, w_rev, _, grad_video, shifts):
    _, n_rows, n_cols, chans = video.shape
    for row in range(n_rows + 2):
        cells = halo_row(row, n_rows, at[1], inner, outer, grad_pre)
        store_shifts(shifts, row, cells.astype(F32))
    step = 4
    for row in range(0, n_rows, step):
        grad_act = None
        for tap in range(3):
            left = shifts[row + tap : row + tap + step].reshape(step * n_cols, 3 * chans)
            term = dot(left, w_rev[3 * chans * tap : 3 * chans * (tap + 1)])
            grad_act = term if grad_act is None else grad_act + term
        cells = video[0, row : row + step].reshape(step * n_cols, chans).astype(F32)
        normed, inv_rms = normalize(cells)
        gate = sigmoid(normed)
        grad_norm = grad_act * (gate * (1.0 + normed * (1.0 - gate)))
        along = jnp.mean(grad_norm * normed, axis=-1, keepdims=True)
        grad_in = inv_rms * (grad_norm - normed * along)
        total = cot[0, row : row + step].reshape(step * n_cols, chans).astype(F32) + grad_in
        grad_video[0, row : row + step] = total.astype(BF16).reshape(step, n_cols, chans)


def output_kernel(at, video, past0, past1, hid0, hid1, hid2, w_t, _, output):
    frame = pl.program_id(0)
    _, n_rows, n_cols, chans = video.shape
    step = 4
    for row in range(0, n_rows, step):
        rows = slice(row, row + step)
        parts = (
            jnp.where(frame < 2, past0[0, rows], hid0[0, rows]),
            jnp.where(frame < 1, past1[0, rows], hid1[0, rows]),
            hid2[0, rows],
        )
        left = jnp.concatenate([part.reshape(step * n_cols, chans) for part in parts], axis=-1)
        cells = video[0, rows].reshape(step * n_cols, chans).astype(F32)
        mixed = dot(left, w_t[...])
        output[0, rows] = (cells + mixed).astype(BF16).reshape(step, n_cols, chans)


def frame_spec(shape, index=lambda f: f):
    return pl.BlockSpec((1,) + tuple(shape[1:]), lambda f, *_: (index(f), 0, 0, 0))


def whole(shape):
    return pl.BlockSpec(
        tuple(shape), lambda f, *_: (0,) * len(shape), pipeline_mode=pl.Buffered(1)
    )


def call(
    body, n_frames, in_specs, out_specs, out_shape, flops, scratch=(), scalars=0, aliases={},
    limit=16,
):
    return pl.pallas_call(
        body,
        grid_spec=pltpu.PrefetchScalarGridSpec(
            num_scalar_prefetch=scalars,
            grid=(n_frames,),
            in_specs=in_specs,
            out_specs=out_specs,
            scratch_shapes=scratch,
        ),
        out_shape=out_shape,
        input_output_aliases=aliases,
        cost_estimate=pl.CostEstimate(flops=flops, bytes_accessed=8 << 20, transcendentals=0),
        compiler_params=pltpu.CompilerParams(vmem_limit_bytes=limit << 20),
    )


def part_of(body, part, parts, specs, out, args, flops, scratch=(), before=None, limit=12):
    count = out.shape[0] // parts
    base = part * count
    in_specs = []
    for shape, index in specs:
        if index is None:
            in_specs.append(whole(shape))
        else:
            in_specs.append(frame_spec(shape, lambda f, g=index: g(f, base)))
    if before is None:
        in_specs.append(pl.BlockSpec(memory_space=pltpu.SMEM))
        before, aliases = jnp.zeros((1,), jnp.int32), {}
    else:
        in_specs.append(pl.BlockSpec(memory_space=pl.ANY))
        aliases = {len(args): 0}
    return call(
        body,
        count,
        in_specs,
        frame_spec(out.shape, lambda f: f + base),
        out,
        flops // parts,
        scratch,
        1,
        aliases,
        limit,
    )(*args, before)


def single(body, out_shapes, flops, *args, limit=12):
    return pl.pallas_call(
        body,
        in_specs=[pl.BlockSpec(memory_space=pltpu.VMEM)] * len(args),
        out_specs=[pl.BlockSpec(memory_space=pltpu.VMEM)] * len(out_shapes),
        out_shape=[jax.ShapeDtypeStruct(shape, BF16) for shape in out_shapes],
        cost_estimate=pl.CostEstimate(flops=flops, bytes_accessed=3 << 20, transcendentals=0),
        compiler_params=pltpu.CompilerParams(vmem_limit_bytes=limit << 20),
    )(*args)


def residual_block(video, spatial_weight, temporal_weight, cotangent):
    _, n_frames, n_rows, n_cols, chans = video.shape
    x, core = lax.axis_index("x"), lax.axis_index("core")
    video, cot = video[0], cotangent[0]
    shape = (n_frames, n_rows, n_cols, chans)
    wide = (n_frames, n_rows + 2, n_cols, 3 * chans)
    edge = (n_frames, 1, n_cols, chans)
    count = n_frames // 2
    half = (count,) + shape[1:]
    pair = 2 * n_frames * n_rows * n_cols * chans * chans
    rows_s, rows_t = spatial_weight.shape[0], temporal_weight.shape[0]
    rows = 8 * (rows_s + rows_t)
    last = n_frames - 1
    at_part = [jnp.stack([x, core, base, last]).astype(jnp.int32) for base in (0, count)]
    same = lambda f, base: f + base

    ahead = along_frames(cot[:2], -1)
    inner, outer = edge_rows(video, core)
    units = both_kernels(spatial_weight, temporal_weight, (x, core))
    shifts = None
    for part in range(2):
        shifts = part_of(
            activate_kernel,
            part,
            2,
            [(shape, same), (edge, same), (edge, same)],
            jax.ShapeDtypeStruct(wide, BF16),
            (at_part[part], video, inner, outer),
            pair,
            before=shifts,
        )
    full_s, full_t = (9 * chans, chans), (3 * chans, chans)
    order = jnp.asarray(unit_order(rows_s, rows_t), BF16)
    w_s, w_t, w_back = single(assemble_kernel, (full_s, full_t, full_t), pair // 4, order, units)
    (w_rev,) = single(reverse_kernel, (full_s,), pair // 4, w_s)

    def cot_specs(base):
        specs = [
            frame_spec(shape, lambda f, k=k: jnp.minimum(f + base + k, last)) for k in range(3)
        ]
        return specs + [
            frame_spec(half, lambda f, k=k: jnp.maximum(f + base + k - last - 1, 0)) for k in (1, 2)
        ]

    forward_shapes = (shape, shape, edge, edge)
    results = ()
    for part in range(2):
        base = part * count
        after = ahead if part else cot
        inputs = 8 + 1
        results = call(
            forward_kernel,
            count,
            [frame_spec(wide, lambda f, base=base: f + base)]
            + cot_specs(base)
            + [whole(full_s), whole(full_t)]
            + [pl.BlockSpec(memory_space=pl.ANY)] * len(results),
            [frame_spec(out, lambda f, base=base: f + base) for out in forward_shapes],
            [jax.ShapeDtypeStruct(out, BF16) for out in forward_shapes],
            12 * pair,
            scalars=1,
            aliases={inputs + i: i for i in range(len(results))},
        )(at_part[part], shifts, cot, cot, cot, after, after, w_s, w_back, *results)
    hidden, grad_pre, edge_in, edge_out = results
    edges = traded_edges(edge_in, edge_out)
    past = along_frames(hidden[count:], 1)
    block, half_block = (2, 2 * rows, chans), (2 * rows, chans)
    block_shapes = (block, half_block, half_block, block, block)
    blocks = call(
        weights_kernel,
        n_frames,
        [frame_spec(wide), frame_spec(shape), frame_spec(shape)] + cot_specs(0),
        [whole(shape_) for shape_ in block_shapes],
        [jax.ShapeDtypeStruct(shape_, F32) for shape_ in block_shapes],
        12 * pair,
        [pltpu.VMEM(full_s, F32), pltpu.VMEM(full_t, F32), pltpu.VMEM((4, 4 * rows, chans), F32)],
        scalars=1,
        limit=26,
    )(at_part[0], shifts, grad_pre, hidden, cot, cot, cot, ahead, ahead)
    grad_video = part_of(
        backward_kernel,
        0,
        1,
        [(shape, same), (edge, same), (edge, same), (shape, same), (shape, same), (full_s, None)],
        jax.ShapeDtypeStruct(shape, BF16),
        (at_part[0], grad_pre, *edges, video, cot, w_rev),
        9 * pair,
        [pltpu.VMEM(wide[1:], BF16)],
    )
    output = part_of(
        output_kernel,
        0,
        1,
        [
            (shape, same),
            (half, lambda f, base: jnp.minimum(f, count - 1)),
            (half, lambda f, base: count - 1),
            (shape, lambda f, base: jnp.maximum(f - 2, 0)),
            (shape, lambda f, base: jnp.maximum(f - 1, 0)),
            (shape, same),
            (full_t, None),
        ],
        jax.ShapeDtypeStruct(shape, BF16),
        (at_part[0], video, past, past, hidden, hidden, hidden, w_t),
        3 * pair,
    )
    spatial_part, temporal_part = summed_kernels(blocks, rows_s, rows_t, core)
    total_cells = n_frames * n_rows * n_cols * lax.axis_size(AXES)
    factor = float(total_cells) ** (-0.5)
    return (output[None], grad_video[None], spatial_part * factor, temporal_part * factor)


def solution(mesh):
    fine = Mesh(mesh.devices.reshape(2, 4, 2, 4, 2), AXES)
    cells = P(None, FRAME_AXES, ROW_AXES, None, None)
    kernels = P(AXES, None)
    return jax.shard_map(
        residual_block,
        mesh=fine,
        in_specs=(cells, kernels, kernels, cells),
        out_specs=(cells, cells, kernels, kernels),
        check_vma=False,
    )
```
